32 devices in a mesh: tm: 16 (over z, y, x), atom: 2 (over core).
Axes of the slice: x: 2, y: 2, z: 4, core: 2. Of those that a mesh axis runs over, the one named last changes fastest.
Arguments:
- positions: int32 [3, 512, 512], P(None, 'tm', 'atom'), may hold values from 0 to 16383, as said below
- velocities: float32 [3, 512, 512], P(None, 'tm', 'atom'), may hold values from -6 to 6
- species: int32 [512], P('atom'), may hold values 0 or 1
- wave_vectors: int32 [3, 256], replicated, may hold values from -64 to 64
Outputs:
- isf: float32 [6, 256, 256], P(None, 'tm', 'atom')
The draws below stay inside these ranges and needn't reach their ends.
Inputs may be any that keep to these rules, and one draw needn't show every extreme that they name: `positions`: coordinates are fixed-point fractions of the periodic box in units of 1/16384.
All inputs are finite; a program needn't handle non-finite values. No bound on the sum of `species` on one device may be relied on, other than what follows from the above.
Results may differ from the reference program's by a relative error of at most 0.0003.
Values sent between devices are 32-bit elements; how exact they have to be, the bound alone decides.
A program may use at most 64 MiB of HBM per device.

```python
import math
import jax
import jax.numpy as jnp
from jax import lax

WAVES = 256
WAVE_MAX = 64
STEP_MAX = 8
ATOMS = 512
FRAMES = 512
LAGS = 256


def draw_positions(key, part):
    start_key = jax.random.fold_in(key, 11)
    step_key = jax.random.fold_in(key, 12)
    anchor = jax.random.randint(start_key, (3, 1, ATOMS), 0, 16384)
    moves = jax.random.randint(step_key, (3, FRAMES, ATOMS), 0 - STEP_MAX, STEP_MAX + 1)
    return jnp.remainder(anchor + jnp.cumsum(moves, axis=1), 16384).astype(jnp.int32)


def touch_ends(values, key, least, high):
    place = [jax.random.randint(jax.random.fold_in(key, axis), (), 0, length) for axis, length in enumerate(values.shape)]
    main_axis = values.shape.index(max(values.shape))
    beside = place[:main_axis] + [(place[main_axis] + 1) % values.shape[main_axis]] + place[main_axis + 1:]
    return values.at[tuple(place)].set(least).at[tuple(beside)].set(high)


def shard_levels(rng, shape, pieces, smallest, largest):
    gain = 1.0
    for position, shards_of in pieces:
        steps = jax.random.uniform(jax.random.fold_in(jax.random.fold_in(rng, 6), position), (shards_of,), jnp.float32, smallest / len(pieces), largest / len(pieces))
        gain = gain * jnp.repeat(jnp.exp(steps), shape[position] // shards_of).reshape((-1,) + (1,) * (len(shape) - 1 - position))
    return gain


def bell_draw(key, shape, width, bound, cuts=(), kind=jnp.bfloat16):
    values = jax.random.normal(key, shape, jnp.float32) * width
    if len(cuts) > 0:
        values = shard_levels(key, shape, cuts, -0.22, 0.18) * values
    return jnp.clip(values, min=-bound, max=bound).astype(kind)


def setup_inputs(seed: int = 0) -> dict:
    key_of = jax.random.split(jax.random.key(seed), 5)
    return {
        "positions": draw_positions(jax.random.fold_in(key_of[4], 71), 0),
        "velocities": bell_draw(key_of[1], (3, FRAMES, ATOMS), 1.0, 6.0, ((1, 16), (2, 2)), jnp.float32),
        "species": touch_ends((jax.random.randint(key_of[2], (ATOMS,), 0, 5) < 1).astype(jnp.int32), jax.random.fold_in(key_of[2], 1), 0, 1),
        "wave_vectors": touch_ends(jax.random.randint(key_of[3], (3, WAVES), 0 - WAVE_MAX, WAVE_MAX + 1), jax.random.fold_in(key_of[3], 1), 0 - WAVE_MAX, WAVE_MAX).astype(jnp.int32),
    }


highest = lax.Precision.HIGHEST


def frame_block(pos_block, vel_block, species_onehot, wave_vectors):
    summed = (pos_block[0][:, :, None] * wave_vectors[0] + pos_block[1][:, :, None] * wave_vectors[1]
              + pos_block[2][:, :, None] * wave_vectors[2])
    angle_unit = jnp.float32(2.0 * math.pi / 16384.0)
    phase = jnp.remainder(summed, 16384).astype(jnp.float32) * angle_unit
    kinds = jnp.concatenate([jnp.ones_like(vel_block[:1]), vel_block], 0)
    weights = kinds[:, None] * species_onehot[None, :, None, :]
    cos_part = jnp.einsum('qsba,bak->qsbk', weights, jnp.cos(phase), precision=highest)
    sin_part = jnp.einsum('qsba,bak->qsbk', weights, jnp.sin(phase), precision=highest)
    return jnp.stack([cos_part, sin_part])


def reference(positions, velocities, species, wave_vectors):
    block_size = 8
    block_count = FRAMES // block_size
    species_onehot = jnp.stack([1 - species, species]).astype(jnp.float32)
    pos_blocks = positions.reshape(3, block_count, block_size, ATOMS).transpose(1, 0, 2, 3)
    vel_blocks = velocities.reshape(3, block_count, block_size, ATOMS).transpose(1, 0, 2, 3)
    raw_modes = lax.map(lambda operands: frame_block(operands[0], operands[1], species_onehot, wave_vectors),
                        (pos_blocks, vel_blocks))
    raw_modes = raw_modes.transpose(1, 2, 3, 0, 4, 5).reshape(2, 4, 2, FRAMES, WAVES)
    wave_scaled = wave_vectors.astype(jnp.float32) / WAVE_MAX
    current = (wave_scaled[0] * raw_modes[:, 1] + wave_scaled[1] * raw_modes[:, 2]
               + wave_scaled[2] * raw_modes[:, 3])
    modes = jnp.stack([raw_modes[:, 0], current], 1)
    signals = jnp.moveaxis(modes, 3, 4)
    spectra = jnp.fft.rfft(signals, n=2 * FRAMES, axis=-1)
    spec_a = spectra[:, :, 0]
    spec_b = spectra[:, :, 1]
    cross = jnp.stack([spec_a * jnp.conj(spec_a), spec_a * jnp.conj(spec_b), spec_b * jnp.conj(spec_b)], 2).sum(0)
    corr = jnp.fft.irfft(cross, n=2 * FRAMES, axis=-1)[..., :LAGS]
    lag_index = jnp.arange(LAGS, dtype=jnp.int32)
    isf = corr / (jnp.float32(ATOMS) * (FRAMES - lag_index).astype(jnp.float32))
    return isf.reshape(6, WAVES, LAGS).astype(jnp.float32)
```

```python
import math

import jax
import jax.numpy as jnp
import ml_dtypes
import numpy as np
from jax import lax
from jax.experimental import pallas as pl
from jax.experimental.pallas import tpu as pltpu
from jax.sharding import PartitionSpec as P

WAVE_MAX = 64


highest = lax.Precision.HIGHEST


def frame_block(pos_block, vel_block, species_onehot, wave_vectors):
    summed = (
        pos_block[0][:, :, None] * wave_vectors[0]
        + pos_block[1][:, :, None] * wave_vectors[1]
        + pos_block[2][:, :, None] * wave_vectors[2]
    )
    angle_unit = jnp.float32(2.0 * math.pi / 16384.0)
    phase = jnp.remainder(summed, 16384).astype(jnp.float32) * angle_unit
    kinds = jnp.concatenate([jnp.ones_like(vel_block[:1]), vel_block], 0)
    weights = kinds[:, None] * species_onehot[None, :, None, :]
    cos_part = jnp.einsum("qsba,bak->qsbk", weights, jnp.cos(phase), precision=highest)
    sin_part = jnp.einsum("qsba,bak->qsbk", weights, jnp.sin(phase), precision=highest)
    return jnp.stack([cos_part, sin_part])


def pair_terms(cos_rows, sin_rows):
    cos_a = cos_rows[:, :, 0]
    cos_b = cos_rows[:, :, 1]
    sin_a = sin_rows[:, :, 0]
    sin_b = sin_rows[:, :, 1]
    real_part = jnp.stack(
        [
            cos_a * cos_a + sin_a * sin_a,
            cos_a * cos_b + sin_a * sin_b,
            cos_b * cos_b + sin_b * sin_b,
        ],
        2,
    ).sum(0)
    imag_part = jnp.stack(
        [
            cos_a * sin_a - sin_a * cos_a,
            cos_a * sin_b - sin_a * cos_b,
            cos_b * sin_b - sin_b * cos_b,
        ],
        2,
    ).sum(0)
    return (real_part, imag_part)


def correlate(signals, atom_total):
    frame_total = signals.shape[-1]
    waves_here = signals.shape[3]
    signal_rows = signals.reshape(-1, frame_total)
    groups = lax.axis_size("atom")
    freq_count = frame_total // groups
    lag_count = frame_total // 2 // groups
    my_index = lax.axis_index("atom")
    freq_index = my_index * freq_count + jnp.arange(freq_count, dtype=jnp.int32)
    time_index = jnp.arange(frame_total, dtype=jnp.int32)
    angle_step = jnp.float32(math.pi / frame_total)
    turns = jnp.remainder(time_index[:, None] * freq_index[None, :], 2 * frame_total)
    angles = turns.astype(jnp.float32) * angle_step
    spec_cos = jnp.dot(signal_rows, jnp.cos(angles), precision=highest).reshape(
        2, 2, 2, waves_here, freq_count
    )
    spec_sin = jnp.dot(signal_rows, jnp.sin(angles), precision=highest).reshape(
        2, 2, 2, waves_here, freq_count
    )
    real_part, imag_part = pair_terms(spec_cos, spec_sin)
    spectral_weight = jnp.where(freq_index == 0, 1.0, 2.0).astype(jnp.float32)
    real_rows = (real_part * spectral_weight).reshape(6 * waves_here, freq_count)
    imag_rows = (imag_part * spectral_weight).reshape(6 * waves_here, freq_count)
    alternating = jnp.where(time_index % 2 == 0, 1.0, -1.0).astype(jnp.float32)
    nyquist = jnp.dot(signal_rows, alternating, precision=highest).reshape(2, 2, 2, waves_here)
    nyq_a = nyquist[:, :, 0]
    nyq_b = nyquist[:, :, 1]
    nyq_real = (
        jnp.stack([nyq_a * nyq_a, nyq_a * nyq_b, nyq_b * nyq_b], 2).sum(0).reshape(6 * waves_here)
    )
    nyq_here = nyq_real * jnp.where(my_index == 0, 1.0, 0.0).astype(jnp.float32)
    lag_index = jnp.arange(lag_count * lax.axis_size("atom"), dtype=jnp.int32)
    lag_turns = jnp.remainder(lag_index[:, None] * freq_index[None, :], 2 * frame_total)
    lag_angles = lag_turns.astype(jnp.float32) * angle_step
    term = jnp.dot(jnp.cos(lag_angles), real_rows.T, precision=highest) - jnp.dot(
        jnp.sin(lag_angles), imag_rows.T, precision=highest
    )
    lag_sign = jnp.where(lag_index % 2 == 0, 1.0, -1.0).astype(jnp.float32)
    shared = lax.psum_scatter(
        term + lag_sign[:, None] * nyq_here[None, :], "atom", scatter_dimension=0, tiled=True
    )
    lag_index = my_index * lag_count + jnp.arange(lag_count, dtype=jnp.int32)
    scaled = shared / jnp.float32(2 * frame_total)
    isf = (
        scaled / (jnp.float32(atom_total) * (frame_total - lag_index).astype(jnp.float32))[:, None]
    )
    return isf.T.reshape(6, waves_here, lag_count)


def per_device_general(positions, velocities, species, wave_vectors):
    atom_count = positions.shape[2]
    frame_count = positions.shape[1]
    wave_count = wave_vectors.shape[1]
    block_size = math.gcd(frame_count, 2)
    block_count = frame_count // block_size
    species_onehot = jnp.stack([1 - species, species]).astype(jnp.float32)
    pos_blocks = positions.reshape(3, block_count, block_size, atom_count).transpose(1, 0, 2, 3)
    vel_blocks = velocities.reshape(3, block_count, block_size, atom_count).transpose(1, 0, 2, 3)
    raw_modes = lax.map(
        lambda operands: frame_block(operands[0], operands[1], species_onehot, wave_vectors),
        (pos_blocks, vel_blocks),
    )
    raw_modes = raw_modes.transpose(1, 2, 3, 0, 4, 5).reshape(2, 4, 2, frame_count, wave_count)
    wave_scaled = wave_vectors.astype(jnp.float32) / WAVE_MAX
    current = (
        wave_scaled[0] * raw_modes[:, 1]
        + wave_scaled[1] * raw_modes[:, 2]
        + wave_scaled[2] * raw_modes[:, 3]
    )
    modes = jnp.stack([raw_modes[:, 0], current], 1)
    atom_groups = lax.axis_size("atom")
    summed = lax.psum(modes, "atom")
    owned = lax.all_to_all(summed, "tm", split_axis=4, concat_axis=3, tiled=True)
    signals = jnp.moveaxis(owned, 3, 4)
    return correlate(signals, atom_count * atom_groups)


GROUP = 16
STEP = 8


def even_coeffs(func, degree):
    fit = np.polynomial.chebyshev.Chebyshev.interpolate(
        lambda z: func(np.sqrt(np.maximum(z, 1e-12))), degree, domain=[0.0, 0.25]
    )
    return [float(v) for v in fit.convert(kind=np.polynomial.Polynomial).coef]


COS_COEFFS = even_coeffs(lambda r: np.sqrt(2.0) * np.cos(np.pi * r), 3)
SIN_COEFFS = even_coeffs(lambda r: np.sqrt(2.0) * np.sin(np.pi * r) / r, 3)


def dft_tables(frames):
    turns = np.outer(np.arange(frames), np.arange(frames)) % (2 * frames)
    angle = turns * (np.pi / frames)
    sine = np.sin(angle)
    sine[:, 0] = 1.0 - 2.0 * (np.arange(frames) % 2)
    table = np.concatenate([np.cos(angle), sine], 1).astype(np.float32)
    high = table.astype(ml_dtypes.bfloat16)
    low = (table - high.astype(np.float32)).astype(ml_dtypes.bfloat16)
    return np.stack([high, low])


def horner(coeffs, z):
    value = coeffs[-1] * z + coeffs[-2]
    for coeff in coeffs[-3::-1]:
        value = value * z + coeff
    return value


def split(value):
    high = value.astype(jnp.bfloat16)
    low = (value - high.astype(jnp.float32)).astype(jnp.bfloat16)
    return high, low


def dot_rows(left, right):
    return lax.dot_general(
        left, right, (((1,), (1,)), ((), ())), preferred_element_type=jnp.float32
    )


def fused_kernel(
    tm_size,
    pos_hbm,
    vel_hbm,
    species_hbm,
    wave_hbm,
    table_hbm,
    out_ref,
    pos_ref,
    vel_ref,
    species_ref,
    wave_ref,
    table,
    wave_cols,
    factor,
    weights,
    acc,
    modes,
    from_pair,
    summed,
    signals,
    result,
    result_in,
    load_sem,
    pair_send,
    pair_recv,
    peer_send,
    peer_recv,
    last_send,
    last_recv,
):
    me = lax.axis_index("tm")
    core = lax.axis_index("atom")
    other = 1 - core
    frames = pos_ref.shape[1]
    waves = wave_ref.shape[1]
    atoms = pos_ref.shape[2]
    groups = frames // GROUP
    frame_total = frames * tm_size
    early = GROUP // STEP // 2

    loads = [
        pltpu.make_async_copy(source, target, load_sem.at[n])
        for n, (source, target) in enumerate(
            (
                (wave_hbm, wave_ref),
                (species_hbm, species_ref),
                (vel_hbm, vel_ref),
                (pos_hbm, pos_ref),
                (table_hbm, table),
            )
        )
    ]
    for load in loads:
        load.start()
    barrier = pltpu.get_barrier_semaphore()
    for hop in range(1, tm_size):
        peer = lax.rem(me + hop, tm_size)
        pl.semaphore_signal(
            barrier, inc=1, device_id=(peer, core), device_id_type=pl.DeviceIdType.MESH
        )
    pl.semaphore_signal(
        barrier, inc=1, device_id=(me, other), device_id_type=pl.DeviceIdType.MESH
    )

    loads[0].wait()
    lane = lax.broadcasted_iota(jnp.int32, (waves, 128), 1)
    for d in range(3):
        row = wave_ref[d : d + 1, :].astype(jnp.float32)
        wave_cols[d] = jnp.broadcast_to(row, (128, waves)).T
    scaled = jnp.where(
        lane < 64, wave_cols[0], jnp.where(lane < 96, wave_cols[1], wave_cols[2])
    ) * (1.0 / WAVE_MAX)
    factor[...] = jnp.where(lane < 32, 1.0, scaled)
    for load in loads[1:4]:
        load.wait()
    species_b = species_ref[...].astype(jnp.float32)
    species_a = 1.0 - species_b

    def trig(t):
        turn = None
        for d in range(3):
            coord = pos_ref[d, pl.ds(t, 1), :].astype(jnp.float32) * (1.0 / 16384.0)
            wave = wave_cols[d]
            term = jnp.concatenate([wave] * (atoms // 128), 1) * coord
            turn = term if turn is None else turn + term
        rest = turn - jnp.round(turn)
        z = rest * rest
        half_sin = rest * horner(SIN_COEFFS, z)
        return 1.0 - half_sin * half_sin, half_sin * horner(COS_COEFFS, z)

    def pair_copy(tg):
        return pltpu.make_async_remote_copy(
            src_ref=modes.at[tg, other],
            dst_ref=from_pair.at[tg],
            send_sem=pair_send.at[tg],
            recv_sem=pair_recv.at[tg],
            device_id=(me, other),
            device_id_type=pl.DeviceIdType.MESH,
        )

    def peer_copy(tg, hop):
        peer = lax.rem(me + hop, tm_size)
        return pltpu.make_async_remote_copy(
            src_ref=summed.at[tg, peer],
            dst_ref=signals.at[me, tg],
            send_sem=peer_send.at[tg, hop],
            recv_sem=peer_recv.at[tg, hop],
            device_id=(peer, core),
            device_id_type=pl.DeviceIdType.MESH,
        )

    def reduce_and_send(tg):
        pair_copy(tg).wait_recv()
        summed[tg] = modes[tg, core] + from_pair[tg]
        for hop in range(1, tm_size):
            peer_copy(tg, hop).start()
        signals[me, tg] = summed[tg, me]

    row_index = lax.broadcasted_iota(jnp.int32, (256, atoms), 0)
    def group(tg, carry):
        rows = []
        for q in range(4):
            for spec in (species_a, species_b):
                if q == 0:
                    rows.append(jnp.broadcast_to(spec, (GROUP, atoms)))
                else:
                    rows.append(vel_ref[q - 1, pl.ds(pl.multiple_of(tg * GROUP, GROUP), GROUP), :] * spec)
        kinds = jnp.concatenate(rows, 0)
        high, low = split(kinds)
        weights[0:128] = high.astype(jnp.float32)
        weights[128:256] = low.astype(jnp.float32)
        acc[...] = jnp.zeros_like(acc)

        def step(index, carry):
            @pl.when(jnp.logical_and(tg == 0, index == GROUP // STEP - 1))
            def _():
                pl.semaphore_wait(barrier, tm_size)

            @pl.when(jnp.logical_and(tg > 0, index == early))
            def _():
                reduce_and_send(tg - 1)

            left_cos, left_sin, right = [], [], []
            for k in range(STEP):
                local = index * STEP + k
                cosine, sine = trig(tg * GROUP + local)
                left_cos += list(split(cosine))
                left_sin += list(split(sine))
                frame_w = jnp.where(
                    (row_index & (GROUP - 1)) == local, weights[...], 0.0
                ).astype(jnp.bfloat16)
                right += [frame_w, frame_w]
            right = jnp.concatenate(right, 1)
            acc[0:waves] += dot_rows(jnp.concatenate(left_cos, 1), right)
            acc[waves : 2 * waves] += dot_rows(jnp.concatenate(left_sin, 1), right)
            return carry

        lax.fori_loop(0, GROUP // STEP, step, 0)
        halves = []
        for c in range(2):
            block = acc[c * waves : (c + 1) * waves]
            part = (block[:, :128] + block[:, 128:]) * factor[...]
            current = part + pltpu.roll(part, 96, 1) + pltpu.roll(part, 64, 1)
            halves.append(jnp.where(lane < 32, part, current))
        packed = jnp.where(lane < 64, halves[0], pltpu.roll(halves[1], 64, 1))
        packed = packed.reshape(tm_size, 2, 8, 128)
        modes[tg, 0] = packed[:, 0]
        modes[tg, 1] = packed[:, 1]
        pair_copy(tg).start()
        return carry

    lax.fori_loop(0, groups, group, 0)
    reduce_and_send(groups - 1)
    loads[4].wait()
    for tg in range(groups):
        for hop in range(1, tm_size):
            peer_copy(tg, hop).wait_recv()

    tiles = signals[...].reshape(frame_total // 128, 8, 8, 128)
    wide = frame_total // 128 * 8
    group_lane = lax.broadcasted_iota(jnp.int32, (wide, 128), 1) // 16
    turned = [
        pltpu.roll(tiles[:, p].reshape(wide, 128), 16 * p, 1) if p else tiles[:, p].reshape(wide, 128)
        for p in range(8)
    ]
    rows = []
    for m in range(8):
        picked = turned[0]
        for p in range(1, 8):
            picked = jnp.where(group_lane == (m + p) % 8, turned[p], picked)
        if m:
            picked = pltpu.roll(picked, 128 - 16 * m, 1)
        rows.append(
            jnp.concatenate([picked[v * 8 : v * 8 + 8] for v in range(frame_total // 128)], 1)
        )
    high, low = split(jnp.concatenate(rows, 0))
    both = jnp.dot(
        jnp.concatenate([high, low], 0), table[0], preferred_element_type=jnp.float32
    )
    spectra = both[:64] + both[64:] + jnp.dot(high, table[1], preferred_element_type=jnp.float32)
    first = lax.broadcasted_iota(jnp.int32, (8, frame_total), 1) == 0
    out_rows = []
    for g in range(2):
        for a, b in ((0, 0), (0, 1), (1, 1)):
            even = jnp.zeros((8, frame_total), jnp.float32)
            odd = jnp.zeros((8, frame_total), jnp.float32)
            imag = jnp.zeros((8, frame_total), jnp.float32)
            for c in range(2):
                row_a = (c * 4 + g * 2 + a) * 8
                row_b = (c * 4 + g * 2 + b) * 8
                cos_a = spectra[row_a : row_a + 8, :frame_total]
                sin_a = spectra[row_a : row_a + 8, frame_total:]
                cos_b = spectra[row_b : row_b + 8, :frame_total]
                sin_b = spectra[row_b : row_b + 8, frame_total:]
                even += cos_a * cos_b
                odd += sin_a * sin_b
                imag += sin_a * cos_b - cos_a * sin_b
            real = jnp.where(first, even, 2.0 * (even + odd))
            imag = jnp.where(first, odd, 2.0 * imag)
            out_rows.append(jnp.concatenate([real, imag], 1))
    high, low = split(jnp.concatenate(out_rows, 0))
    lags = 2 * out_ref.shape[2]
    both = dot_rows(jnp.concatenate([high, low], 0), table[0, :lags])
    corr = both[:48] + both[48:] + dot_rows(high, table[1, :lags])
    lag = lax.broadcasted_iota(jnp.int32, (1, lags), 1)
    norm = 1.0 / (
        (frame_total - lag).astype(jnp.float32) * jnp.float32(2 * frame_total * 2 * atoms)
    )
    corr = (corr * norm).reshape(6, 8, lags)
    result[0] = corr[:, :, : lags // 2]
    result[1] = corr[:, :, lags // 2 :]
    swap = pltpu.make_async_remote_copy(
        src_ref=result.at[other],
        dst_ref=result_in,
        send_sem=last_send,
        recv_sem=last_recv,
        device_id=(me, other),
        device_id_type=pl.DeviceIdType.MESH,
    )
    swap.start()
    out_ref[:, pl.ds(pl.multiple_of(core * 8, 8), 8), :] = result[core]
    for tg in range(groups):
        pair_copy(tg).wait_send()
        for hop in range(1, tm_size):
            peer_copy(tg, hop).wait_send()
    swap.wait()
    out_ref[:, pl.ds(pl.multiple_of(other * 8, 8), 8), :] = result_in[...]


def per_device_fused(tm_size, positions, velocities, species, wave_vectors):
    frames, atoms = positions.shape[1:]
    waves = wave_vectors.shape[1]
    groups = frames // GROUP
    frame_total = frames * tm_size
    lag_here = frame_total // 4
    vmem = pl.BlockSpec(memory_space=pltpu.VMEM)
    dma = pltpu.SemaphoreType.DMA
    return pl.pallas_call(
        lambda *refs: fused_kernel(tm_size, *refs),
        name="scattering",
        out_shape=jax.ShapeDtypeStruct((6, 16, lag_here), jnp.float32),
        in_specs=[pl.BlockSpec(memory_space=pltpu.HBM)] * 5,
        out_specs=vmem,
        scratch_shapes=[
            pltpu.VMEM(positions.shape, jnp.int32),
            pltpu.VMEM(velocities.shape, jnp.float32),
            pltpu.VMEM((1, atoms), jnp.int32),
            pltpu.VMEM(wave_vectors.shape, jnp.int32),
            pltpu.VMEM((2, frame_total, 2 * frame_total), jnp.bfloat16),
            pltpu.VMEM((3, waves, 128), jnp.float32),
            pltpu.VMEM((waves, 128), jnp.float32),
            pltpu.VMEM((256, atoms), jnp.float32),
            pltpu.VMEM((2 * waves, 256), jnp.float32),
            pltpu.VMEM((groups, 2, tm_size, 8, 128), jnp.float32),
            pltpu.VMEM((groups, tm_size, 8, 128), jnp.float32),
            pltpu.VMEM((groups, tm_size, 8, 128), jnp.float32),
            pltpu.VMEM((tm_size, groups, 8, 128), jnp.float32),
            pltpu.VMEM((2, 6, 8, lag_here), jnp.float32),
            pltpu.VMEM((6, 8, lag_here), jnp.float32),
            dma((5,)),
            dma((groups,)),
            dma((groups,)),
            dma((groups, tm_size)),
            dma((groups, tm_size)),
            dma,
            dma,
        ],
        compiler_params=pltpu.CompilerParams(
            collective_id=0, has_side_effects=True, vmem_limit_bytes=48 << 20
        ),
    )(
        *(
            pltpu.with_memory_space_constraint(operand, pltpu.HBM)
            for operand in (
                positions,
                velocities,
                species.reshape(1, atoms),
                wave_vectors,
                jnp.asarray(dft_tables(frame_total)),
            )
        )
    )


def solution(mesh):
    tm_size = mesh.shape["tm"]
    atom_size = mesh.shape["atom"]

    def per_device(positions, velocities, species, wave_vectors):
        frames, atoms = positions.shape[1:]
        waves = wave_vectors.shape[1]
        fits = (
            tm_size == 16
            and atom_size == 2
            and frames == 2 * GROUP
            and atoms == 256
            and waves == 256
        )
        if fits:
            return per_device_fused(tm_size, positions, velocities, species, wave_vectors)
        return per_device_general(positions, velocities, species, wave_vectors)

    return jax.shard_map(
        per_device,
        mesh=mesh,
        in_specs=(P(None, "tm", "atom"), P(None, "tm", "atom"), P("atom"), P()),
        out_specs=P(None, "tm", "atom"),
        check_vma=False,
    )
```

```python
import math

import jax
import jax.numpy as jnp
import ml_dtypes
import numpy as np
from jax import lax
from jax.experimental import pallas as pl
from jax.experimental.pallas import tpu as pltpu
from jax.sharding import PartitionSpec as P

WAVE_MAX = 64


highest = lax.Precision.HIGHEST


def frame_block(pos_block, vel_block, species_onehot, wave_vectors):
    summed = (
        pos_block[0][:, :, None] * wave_vectors[0]
        + pos_block[1][:, :, None] * wave_vectors[1]
        + pos_block[2][:, :, None] * wave_vectors[2]
    )
    angle_unit = jnp.float32(2.0 * math.pi / 16384.0)
    phase = jnp.remainder(summed, 16384).astype(jnp.float32) * angle_unit
    kinds = jnp.concatenate([jnp.ones_like(vel_block[:1]), vel_block], 0)
    weights = kinds[:, None] * species_onehot[None, :, None, :]
    cos_part = jnp.einsum("qsba,bak->qsbk", weights, jnp.cos(phase), precision=highest)
    sin_part = jnp.einsum("qsba,bak->qsbk", weights, jnp.sin(phase), precision=highest)
    return jnp.stack([cos_part, sin_part])


def pair_terms(cos_rows, sin_rows):
    cos_a = cos_rows[:, :, 0]
    cos_b = cos_rows[:, :, 1]
    sin_a = sin_rows[:, :, 0]
    sin_b = sin_rows[:, :, 1]
    real_part = jnp.stack(
        [
            cos_a * cos_a + sin_a * sin_a,
            cos_a * cos_b + sin_a * sin_b,
            cos_b * cos_b + sin_b * sin_b,
        ],
        2,
    ).sum(0)
    imag_part = jnp.stack(
        [
            cos_a * sin_a - sin_a * cos_a,
            cos_a * sin_b - sin_a * cos_b,
            cos_b * sin_b - sin_b * cos_b,
        ],
        2,
    ).sum(0)
    return (real_part, imag_part)


def correlate(signals, atom_total):
    frame_total = signals.shape[-1]
    waves_here = signals.shape[3]
    signal_rows = signals.reshape(-1, frame_total)
    groups = lax.axis_size("atom")
    freq_count = frame_total // groups
    lag_count = frame_total // 2 // groups
    my_index = lax.axis_index("atom")
    freq_index = my_index * freq_count + jnp.arange(freq_count, dtype=jnp.int32)
    time_index = jnp.arange(frame_total, dtype=jnp.int32)
    angle_step = jnp.float32(math.pi / frame_total)
    turns = jnp.remainder(time_index[:, None] * freq_index[None, :], 2 * frame_total)
    angles = turns.astype(jnp.float32) * angle_step
    spec_cos = jnp.dot(signal_rows, jnp.cos(angles), precision=highest).reshape(
        2, 2, 2, waves_here, freq_count
    )
    spec_sin = jnp.dot(signal_rows, jnp.sin(angles), precision=highest).reshape(
        2, 2, 2, waves_here, freq_count
    )
    real_part, imag_part = pair_terms(spec_cos, spec_sin)
    spectral_weight = jnp.where(freq_index == 0, 1.0, 2.0).astype(jnp.float32)
    real_rows = (real_part * spectral_weight).reshape(6 * waves_here, freq_count)
    imag_rows = (imag_part * spectral_weight).reshape(6 * waves_here, freq_count)
    alternating = jnp.where(time_index % 2 == 0, 1.0, -1.0).astype(jnp.float32)
    nyquist = jnp.dot(signal_rows, alternating, precision=highest).reshape(2, 2, 2, waves_here)
    nyq_a = nyquist[:, :, 0]
    nyq_b = nyquist[:, :, 1]
    nyq_real = (
        jnp.stack([nyq_a * nyq_a, nyq_a * nyq_b, nyq_b * nyq_b], 2).sum(0).reshape(6 * waves_here)
    )
    nyq_here = nyq_real * jnp.where(my_index == 0, 1.0, 0.0).astype(jnp.float32)
    lag_index = jnp.arange(lag_count * lax.axis_size("atom"), dtype=jnp.int32)
    lag_turns = jnp.remainder(lag_index[:, None] * freq_index[None, :], 2 * frame_total)
    lag_angles = lag_turns.astype(jnp.float32) * angle_step
    term = jnp.dot(jnp.cos(lag_angles), real_rows.T, precision=highest) - jnp.dot(
        jnp.sin(lag_angles), imag_rows.T, precision=highest
    )
    lag_sign = jnp.where(lag_index % 2 == 0, 1.0, -1.0).astype(jnp.float32)
    shared = lax.psum_scatter(
        term + lag_sign[:, None] * nyq_here[None, :], "atom", scatter_dimension=0, tiled=True
    )
    lag_index = my_index * lag_count + jnp.arange(lag_count, dtype=jnp.int32)
    scaled = shared / jnp.float32(2 * frame_total)
    isf = (
        scaled / (jnp.float32(atom_total) * (frame_total - lag_index).astype(jnp.float32))[:, None]
    )
    return isf.T.reshape(6, waves_here, lag_count)


def per_device_general(positions, velocities, species, wave_vectors):
    atom_count = positions.shape[2]
    frame_count = positions.shape[1]
    wave_count = wave_vectors.shape[1]
    block_size = math.gcd(frame_count, 2)
    block_count = frame_count // block_size
    species_onehot = jnp.stack([1 - species, species]).astype(jnp.float32)
    pos_blocks = positions.reshape(3, block_count, block_size, atom_count).transpose(1, 0, 2, 3)
    vel_blocks = velocities.reshape(3, block_count, block_size, atom_count).transpose(1, 0, 2, 3)
    raw_modes = lax.map(
        lambda operands: frame_block(operands[0], operands[1], species_onehot, wave_vectors),
        (pos_blocks, vel_blocks),
    )
    raw_modes = raw_modes.transpose(1, 2, 3, 0, 4, 5).reshape(2, 4, 2, frame_count, wave_count)
    wave_scaled = wave_vectors.astype(jnp.float32) / WAVE_MAX
    current = (
        wave_scaled[0] * raw_modes[:, 1]
        + wave_scaled[1] * raw_modes[:, 2]
        + wave_scaled[2] * raw_modes[:, 3]
    )
    modes = jnp.stack([raw_modes[:, 0], current], 1)
    atom_groups = lax.axis_size("atom")
    summed = lax.psum(modes, "atom")
    owned = lax.all_to_all(summed, "tm", split_axis=4, concat_axis=3, tiled=True)
    signals = jnp.moveaxis(owned, 3, 4)
    return correlate(signals, atom_count * atom_groups)


GROUP = 16
STEP = 4


def even_coeffs(func, degree):
    fit = np.polynomial.chebyshev.Chebyshev.interpolate(
        lambda z: func(np.sqrt(np.maximum(z, 1e-12))), degree, domain=[0.0, 0.25]
    )
    return [float(v) for v in fit.convert(kind=np.polynomial.Polynomial).coef]


def monic_cubic(coeffs):
    scale = coeffs[3]
    low, mid, high = (c / scale for c in coeffs[:3])
    return scale, high, mid, low - high * mid


COS_SCALE, COS_A, COS_B, COS_C = monic_cubic(
    even_coeffs(lambda r: np.sqrt(2.0) * np.cos(np.pi * r), 3)
)
SIN_SCALE, SIN_A, SIN_B, SIN_C = monic_cubic(
    even_coeffs(lambda r: np.sqrt(2.0) * np.sin(np.pi * r) / r, 3)
)


def dft_tables(frames):
    turns = np.outer(np.arange(frames), np.arange(frames)) % (2 * frames)
    angle = turns * (np.pi / frames)
    sine = np.sin(angle)
    sine[:, 0] = 1.0 - 2.0 * (np.arange(frames) % 2)
    table = np.concatenate([np.cos(angle), sine], 1).astype(np.float32)
    high = table.astype(ml_dtypes.bfloat16)
    low = (table - high.astype(np.float32)).astype(ml_dtypes.bfloat16)
    return np.stack([high, low])


def split(value):
    high = value.astype(jnp.bfloat16)
    low = (value - high.astype(jnp.float32)).astype(jnp.bfloat16)
    return high, low


def dot_rows(left, right):
    return lax.dot_general(
        left, right, (((1,), (1,)), ((), ())), preferred_element_type=jnp.float32
    )


def fused_kernel(
    tm_size,
    pos_hbm,
    vel_hbm,
    species_hbm,
    wave_hbm,
    table_hbm,
    out_ref,
    pos_ref,
    vel_ref,
    species_ref,
    wave_ref,
    table,
    wave_mat,
    coords,
    places,
    kinds,
    turns,
    acc,
    modes,
    from_pair,
    summed,
    signals,
    result,
    result_in,
    load_sem,
    pair_send,
    pair_recv,
    peer_send,
    peer_recv,
    last_send,
    last_recv,
):
    me = lax.axis_index("tm")
    core = lax.axis_index("atom")
    other = 1 - core
    frames = pos_ref.shape[1]
    waves = wave_ref.shape[1]
    atoms = pos_ref.shape[2]
    groups = frames // GROUP
    frame_total = frames * tm_size
    early = GROUP // STEP // 2

    loads = [
        pltpu.make_async_copy(source, target, load_sem.at[n])
        for n, (source, target) in enumerate(
            (
                (wave_hbm, wave_ref),
                (species_hbm, species_ref),
                (vel_hbm, vel_ref),
                (pos_hbm, pos_ref),
                (table_hbm, table),
            )
        )
    ]
    for load in loads:
        load.start()
    barrier = pltpu.get_barrier_semaphore()
    for hop in range(1, tm_size):
        peer = lax.rem(me + hop, tm_size)
        pl.semaphore_signal(
            barrier, inc=1, device_id=(peer, core), device_id_type=pl.DeviceIdType.MESH
        )
    pl.semaphore_signal(
        barrier, inc=1, device_id=(me, other), device_id_type=pl.DeviceIdType.MESH
    )

    loads[0].wait()
    waves_f = wave_ref[...].astype(jnp.float32)
    eight = jnp.concatenate(
        [waves_f[d : d + 1] for d in (0, 0, 1, 1, 2, 2)] + [jnp.zeros((2, waves), jnp.float32)], 0
    )
    none = jnp.zeros_like(eight)
    wave_mat[...] = jnp.zeros_like(wave_mat)
    for t in range(GROUP):
        pair = [none, eight] if t % 2 else [eight, none]
        wave_mat[t, t // 2 * 16 : t // 2 * 16 + 16] = jnp.concatenate(pair, 0).astype(jnp.bfloat16)
    for load in loads[1:4]:
        load.wait()

    def scatter(target, place, value):
        for n in range(2):
            target[n, pl.ds(place, frames, stride=8), :] = value[:, n * 128 : n * 128 + 128]

    for d in range(3):
        x = pos_ref[d]
        scatter(coords, 2 * d, (x >> 7).astype(jnp.float32) * (1.0 / 128.0))
        scatter(coords, 2 * d + 1, (x & 127).astype(jnp.float32) * (1.0 / 16384.0))
    for d in (6, 7):
        scatter(coords, d, jnp.zeros((frames, atoms), jnp.float32))
    species_b = species_ref[...].astype(jnp.float32)
    species_a = 1.0 - species_b
    for q in range(4):
        for n, spec in enumerate((species_a, species_b)):
            if q == 0:
                rows = jnp.broadcast_to(spec, (frames, atoms))
            else:
                rows = vel_ref[q - 1] * spec
            scatter(kinds, 2 * q + n, rows)

    def trig(turn):
        rest = turn - jnp.round(turn)
        z = rest * rest
        zz = z * z
        half_sin = rest * ((z + SIN_A) * (zz + SIN_B) + SIN_C)
        half_cos = (z + COS_A) * (zz + COS_B) + COS_C
        return half_sin * half_sin, half_sin * half_cos

    def pair_copy(tg):
        return pltpu.make_async_remote_copy(
            src_ref=modes.at[tg, other],
            dst_ref=from_pair.at[tg],
            send_sem=pair_send.at[tg],
            recv_sem=pair_recv.at[tg],
            device_id=(me, other),
            device_id_type=pl.DeviceIdType.MESH,
        )

    def peer_copy(tg, hop):
        peer = lax.rem(me + hop, tm_size)
        return pltpu.make_async_remote_copy(
            src_ref=summed.at[tg, peer],
            dst_ref=signals.at[me, tg],
            send_sem=peer_send.at[tg, hop],
            recv_sem=peer_recv.at[tg, hop],
            device_id=(peer, core),
            device_id_type=pl.DeviceIdType.MESH,
        )

    def reduce_and_send(tg):
        pair_copy(tg).wait_recv()
        summed[tg] = modes[tg, core] + from_pair[tg]
        for hop in range(1, tm_size):
            peer_copy(tg, hop).start()
        signals[me, tg] = summed[tg, me]

    half = atoms // 2

    def find_turn(local, slot):
        turns[slot] = jnp.dot(
            places[...], wave_mat[local & (GROUP - 1)], preferred_element_type=jnp.float32
        )

    def one_frame(tg, local, slot):
        first = pl.multiple_of(local * 8, 8)
        rows = pl.ds(pl.multiple_of(tg * GROUP * 8 + first, 8), 8)
        kind = jnp.concatenate([kinds[0, rows, :], kinds[1, rows, :]], 1)
        total = jnp.sum(kind, axis=1, keepdims=True)
        kind_high = kind.astype(jnp.bfloat16).astype(jnp.float32)
        weight = jnp.concatenate([kind_high, kind - kind_high], 0).astype(jnp.bfloat16)
        sums = [None, None]
        for n in range(2):
            left = weight[:, n * half : n * half + half]
            left = jnp.concatenate([left, left], 1)
            for c, value in enumerate(trig(turns[slot, n * half : n * half + half])):
                part = jnp.dot(
                    left,
                    jnp.concatenate(split(value), 0),
                    preferred_element_type=jnp.float32,
                )
                sums[c] = part if n == 0 else sums[c] + part
        drop, sine = (v[:8] + v[8:] for v in sums)
        cosine = total - (SIN_SCALE * SIN_SCALE) * drop
        sine = (SIN_SCALE * COS_SCALE) * sine
        for n in range(2):
            acc[0, n, pl.ds(first, 8), :] = cosine[:, n * 128 : n * 128 + 128]
            acc[1, n, pl.ds(first, 8), :] = sine[:, n * 128 : n * 128 + 128]

    def group(tg, carry):
        for n in range(2):
            block = coords[n, pl.ds(pl.multiple_of(tg * GROUP * 8, GROUP * 8), GROUP * 8), :]
            places[n * 128 : n * 128 + 128] = block.T.astype(jnp.bfloat16)
        find_turn(0, 0)

        def step(index, carry):
            @pl.when(jnp.logical_and(tg == 0, index == GROUP // STEP - 1))
            def _():
                pl.semaphore_wait(barrier, tm_size)

            @pl.when(jnp.logical_and(tg > 0, index == early))
            def _():
                reduce_and_send(tg - 1)

            for k in range(STEP):
                local = index * STEP + k
                find_turn(local + 1, (k + 1) % 2)
                one_frame(tg, local, k % 2)
            return carry

        lax.fori_loop(0, GROUP // STEP, step, 0)
        factors = wave_ref[...].astype(jnp.float32) * (1.0 / WAVE_MAX)
        rows = []
        for c in range(2):
            part = [
                jnp.concatenate([acc[c, m, pl.ds(n, GROUP, stride=8), :] for m in range(2)], 1)
                for n in range(8)
            ]
            rows += part[:2]
            for n in range(2):
                rows.append(
                    factors[0:1] * part[2 + n]
                    + factors[1:2] * part[4 + n]
                    + factors[2:3] * part[6 + n]
                )
        packed = jnp.concatenate(rows, 0).T.reshape(tm_size, 2, 8, 128)
        modes[tg, 0] = packed[:, 0]
        modes[tg, 1] = packed[:, 1]
        pair_copy(tg).start()
        return carry

    lax.fori_loop(0, groups, group, 0)
    reduce_and_send(groups - 1)
    loads[4].wait()
    for tg in range(groups):
        for hop in range(1, tm_size):
            peer_copy(tg, hop).wait_recv()

    tiles = signals[...].reshape(frame_total // 128, 8, 8, 128)
    wide = frame_total // 128 * 8
    group_lane = lax.broadcasted_iota(jnp.int32, (wide, 128), 1) // 16
    turned = [
        pltpu.roll(tiles[:, p].reshape(wide, 128), 16 * p, 1) if p else tiles[:, p].reshape(wide, 128)
        for p in range(8)
    ]
    rows = []
    for m in range(8):
        picked = turned[0]
        for p in range(1, 8):
            picked = jnp.where(group_lane == (m + p) % 8, turned[p], picked)
        if m:
            picked = pltpu.roll(picked, 128 - 16 * m, 1)
        rows.append(
            jnp.concatenate([picked[v * 8 : v * 8 + 8] for v in range(frame_total // 128)], 1)
        )
    high, low = split(jnp.concatenate(rows, 0))
    both = jnp.dot(
        jnp.concatenate([high, low], 0), table[0], preferred_element_type=jnp.float32
    )
    spectra = both[:64] + both[64:] + jnp.dot(high, table[1], preferred_element_type=jnp.float32)
    first = lax.broadcasted_iota(jnp.int32, (8, frame_total), 1) == 0
    out_rows = []
    for g in range(2):
        for a, b in ((0, 0), (0, 1), (1, 1)):
            even = jnp.zeros((8, frame_total), jnp.float32)
            odd = jnp.zeros((8, frame_total), jnp.float32)
            imag = jnp.zeros((8, frame_total), jnp.float32)
            for c in range(2):
                row_a = (c * 4 + g * 2 + a) * 8
                row_b = (c * 4 + g * 2 + b) * 8
                cos_a = spectra[row_a : row_a + 8, :frame_total]
                sin_a = spectra[row_a : row_a + 8, frame_total:]
                cos_b = spectra[row_b : row_b + 8, :frame_total]
                sin_b = spectra[row_b : row_b + 8, frame_total:]
                even += cos_a * cos_b
                odd += sin_a * sin_b
                imag += sin_a * cos_b - cos_a * sin_b
            real = jnp.where(first, even, 2.0 * (even + odd))
            imag = jnp.where(first, odd, 2.0 * imag)
            out_rows.append(jnp.concatenate([real, imag], 1))
    high, low = split(jnp.concatenate(out_rows, 0))
    lags = 2 * out_ref.shape[2]
    both = dot_rows(jnp.concatenate([high, low], 0), table[0, :lags])
    corr = both[:48] + both[48:] + dot_rows(high, table[1, :lags])
    lag = lax.broadcasted_iota(jnp.int32, (1, lags), 1)
    norm = 1.0 / (
        (frame_total - lag).astype(jnp.float32) * jnp.float32(2 * frame_total * 2 * atoms)
    )
    corr = (corr * norm).reshape(6, 8, lags)
    result[0] = corr[:, :, : lags // 2]
    result[1] = corr[:, :, lags // 2 :]
    swap = pltpu.make_async_remote_copy(
        src_ref=result.at[other],
        dst_ref=result_in,
        send_sem=last_send,
        recv_sem=last_recv,
        device_id=(me, other),
        device_id_type=pl.DeviceIdType.MESH,
    )
    swap.start()
    out_ref[:, pl.ds(pl.multiple_of(core * 8, 8), 8), :] = result[core]
    for tg in range(groups):
        pair_copy(tg).wait_send()
        for hop in range(1, tm_size):
            peer_copy(tg, hop).wait_send()
    swap.wait()
    out_ref[:, pl.ds(pl.multiple_of(other * 8, 8), 8), :] = result_in[...]


def per_device_fused(tm_size, positions, velocities, species, wave_vectors):
    frames, atoms = positions.shape[1:]
    waves = wave_vectors.shape[1]
    groups = frames // GROUP
    frame_total = frames * tm_size
    lag_here = frame_total // 4
    vmem = pl.BlockSpec(memory_space=pltpu.VMEM)
    dma = pltpu.SemaphoreType.DMA
    return pl.pallas_call(
        lambda *refs: fused_kernel(tm_size, *refs),
        name="scattering",
        out_shape=jax.ShapeDtypeStruct((6, 16, lag_here), jnp.float32),
        in_specs=[pl.BlockSpec(memory_space=pltpu.HBM)] * 5,
        out_specs=vmem,
        scratch_shapes=[
            pltpu.VMEM(positions.shape, jnp.int32),
            pltpu.VMEM(velocities.shape, jnp.float32),
            pltpu.VMEM((1, atoms), jnp.int32),
            pltpu.VMEM(wave_vectors.shape, jnp.int32),
            pltpu.VMEM((2, frame_total, 2 * frame_total), jnp.bfloat16),
            pltpu.VMEM((GROUP, 8 * GROUP, waves), jnp.bfloat16),
            pltpu.VMEM((2, 8 * frames, 128), jnp.float32),
            pltpu.VMEM((atoms, 8 * GROUP), jnp.bfloat16),
            pltpu.VMEM((2, 8 * frames, 128), jnp.float32),
            pltpu.VMEM((2, atoms, waves), jnp.float32),
            pltpu.VMEM((2, 2, 8 * GROUP, 128), jnp.float32),
            pltpu.VMEM((groups, 2, tm_size, 8, 128), jnp.float32),
            pltpu.VMEM((groups, tm_size, 8, 128), jnp.float32),
            pltpu.VMEM((groups, tm_size, 8, 128), jnp.float32),
            pltpu.VMEM((tm_size, groups, 8, 128), jnp.float32),
            pltpu.VMEM((2, 6, 8, lag_here), jnp.float32),
            pltpu.VMEM((6, 8, lag_here), jnp.float32),
            dma((5,)),
            dma((groups,)),
            dma((groups,)),
            dma((groups, tm_size)),
            dma((groups, tm_size)),
            dma,
            dma,
        ],
        compiler_params=pltpu.CompilerParams(
            collective_id=0, has_side_effects=True, vmem_limit_bytes=48 << 20
        ),
    )(
        *(
            pltpu.with_memory_space_constraint(operand, pltpu.HBM)
            for operand in (
                positions,
                velocities,
                species.reshape(1, atoms),
                wave_vectors,
                jnp.asarray(dft_tables(frame_total)),
            )
        )
    )


def solution(mesh):
    tm_size = mesh.shape["tm"]
    atom_size = mesh.shape["atom"]

    def per_device(positions, velocities, species, wave_vectors):
        frames, atoms = positions.shape[1:]
        waves = wave_vectors.shape[1]
        fits = (
            tm_size == 16
            and atom_size == 2
            and frames == 2 * GROUP
            and atoms == 256
            and waves == 256
        )
        if fits:
            return per_device_fused(tm_size, positions, velocities, species, wave_vectors)
        return per_device_general(positions, velocities, species, wave_vectors)

    return jax.shard_map(
        per_device,
        mesh=mesh,
        in_specs=(P(None, "tm", "atom"), P(None, "tm", "atom"), P("atom"), P()),
        out_specs=P(None, "tm", "atom"),
        check_vma=False,
    )
```

```python
import math

import jax
import jax.numpy as jnp
import ml_dtypes
import numpy as np
from jax import lax
from jax.experimental import pallas as pl
from jax.experimental.pallas import tpu as pltpu
from jax.sharding import PartitionSpec as P

WAVE_MAX = 64


highest = lax.Precision.HIGHEST


def frame_block(pos_block, vel_block, species_onehot, wave_vectors):
    summed = (
        pos_block[0][:, :, None] * wave_vectors[0]
        + pos_block[1][:, :, None] * wave_vectors[1]
        + pos_block[2][:, :, None] * wave_vectors[2]
    )
    angle_unit = jnp.float32(2.0 * math.pi / 16384.0)
    phase = jnp.remainder(summed, 16384).astype(jnp.float32) * angle_unit
    kinds = jnp.concatenate([jnp.ones_like(vel_block[:1]), vel_block], 0)
    weights = kinds[:, None] * species_onehot[None, :, None, :]
    cos_part = jnp.einsum("qsba,bak->qsbk", weights, jnp.cos(phase), precision=highest)
    sin_part = jnp.einsum("qsba,bak->qsbk", weights, jnp.sin(phase), precision=highest)
    return jnp.stack([cos_part, sin_part])


def pair_terms(cos_rows, sin_rows):
    cos_a = cos_rows[:, :, 0]
    cos_b = cos_rows[:, :, 1]
    sin_a = sin_rows[:, :, 0]
    sin_b = sin_rows[:, :, 1]
    real_part = jnp.stack(
        [
            cos_a * cos_a + sin_a * sin_a,
            cos_a * cos_b + sin_a * sin_b,
            cos_b * cos_b + sin_b * sin_b,
        ],
        2,
    ).sum(0)
    imag_part = jnp.stack(
        [
            cos_a * sin_a - sin_a * cos_a,
            cos_a * sin_b - sin_a * cos_b,
            cos_b * sin_b - sin_b * cos_b,
        ],
        2,
    ).sum(0)
    return (real_part, imag_part)


def correlate(signals, atom_total):
    frame_total = signals.shape[-1]
    waves_here = signals.shape[3]
    signal_rows = signals.reshape(-1, frame_total)
    groups = lax.axis_size("atom")
    freq_count = frame_total // groups
    lag_count = frame_total // 2 // groups
    my_index = lax.axis_index("atom")
    freq_index = my_index * freq_count + jnp.arange(freq_count, dtype=jnp.int32)
    time_index = jnp.arange(frame_total, dtype=jnp.int32)
    angle_step = jnp.float32(math.pi / frame_total)
    turns = jnp.remainder(time_index[:, None] * freq_index[None, :], 2 * frame_total)
    angles = turns.astype(jnp.float32) * angle_step
    spec_cos = jnp.dot(signal_rows, jnp.cos(angles), precision=highest).reshape(
        2, 2, 2, waves_here, freq_count
    )
    spec_sin = jnp.dot(signal_rows, jnp.sin(angles), precision=highest).reshape(
        2, 2, 2, waves_here, freq_count
    )
    real_part, imag_part = pair_terms(spec_cos, spec_sin)
    spectral_weight = jnp.where(freq_index == 0, 1.0, 2.0).astype(jnp.float32)
    real_rows = (real_part * spectral_weight).reshape(6 * waves_here, freq_count)
    imag_rows = (imag_part * spectral_weight).reshape(6 * waves_here, freq_count)
    alternating = jnp.where(time_index % 2 == 0, 1.0, -1.0).astype(jnp.float32)
    nyquist = jnp.dot(signal_rows, alternating, precision=highest).reshape(2, 2, 2, waves_here)
    nyq_a = nyquist[:, :, 0]
    nyq_b = nyquist[:, :, 1]
    nyq_real = (
        jnp.stack([nyq_a * nyq_a, nyq_a * nyq_b, nyq_b * nyq_b], 2).sum(0).reshape(6 * waves_here)
    )
    nyq_here = nyq_real * jnp.where(my_index == 0, 1.0, 0.0).astype(jnp.float32)
    lag_index = jnp.arange(lag_count * lax.axis_size("atom"), dtype=jnp.int32)
    lag_turns = jnp.remainder(lag_index[:, None] * freq_index[None, :], 2 * frame_total)
    lag_angles = lag_turns.astype(jnp.float32) * angle_step
    term = jnp.dot(jnp.cos(lag_angles), real_rows.T, precision=highest) - jnp.dot(
        jnp.sin(lag_angles), imag_rows.T, precision=highest
    )
    lag_sign = jnp.where(lag_index % 2 == 0, 1.0, -1.0).astype(jnp.float32)
    shared = lax.psum_scatter(
        term + lag_sign[:, None] * nyq_here[None, :], "atom", scatter_dimension=0, tiled=True
    )
    lag_index = my_index * lag_count + jnp.arange(lag_count, dtype=jnp.int32)
    scaled = shared / jnp.float32(2 * frame_total)
    isf = (
        scaled / (jnp.float32(atom_total) * (frame_total - lag_index).astype(jnp.float32))[:, None]
    )
    return isf.T.reshape(6, waves_here, lag_count)


def per_device_general(positions, velocities, species, wave_vectors):
    atom_count = positions.shape[2]
    frame_count = positions.shape[1]
    wave_count = wave_vectors.shape[1]
    block_size = math.gcd(frame_count, 2)
    block_count = frame_count // block_size
    species_onehot = jnp.stack([1 - species, species]).astype(jnp.float32)
    pos_blocks = positions.reshape(3, block_count, block_size, atom_count).transpose(1, 0, 2, 3)
    vel_blocks = velocities.reshape(3, block_count, block_size, atom_count).transpose(1, 0, 2, 3)
    raw_modes = lax.map(
        lambda operands: frame_block(operands[0], operands[1], species_onehot, wave_vectors),
        (pos_blocks, vel_blocks),
    )
    raw_modes = raw_modes.transpose(1, 2, 3, 0, 4, 5).reshape(2, 4, 2, frame_count, wave_count)
    wave_scaled = wave_vectors.astype(jnp.float32) / WAVE_MAX
    current = (
        wave_scaled[0] * raw_modes[:, 1]
        + wave_scaled[1] * raw_modes[:, 2]
        + wave_scaled[2] * raw_modes[:, 3]
    )
    modes = jnp.stack([raw_modes[:, 0], current], 1)
    atom_groups = lax.axis_size("atom")
    summed = lax.psum(modes, "atom")
    owned = lax.all_to_all(summed, "tm", split_axis=4, concat_axis=3, tiled=True)
    signals = jnp.moveaxis(owned, 3, 4)
    return correlate(signals, atom_count * atom_groups)


GROUP = 16
STEP = 4
BLOCK = 128
SEND_STEP = 1


def even_coeffs(func, degree):
    fit = np.polynomial.chebyshev.Chebyshev.interpolate(
        lambda z: func(np.sqrt(np.maximum(z, 1e-12))), degree, domain=[0.0, 0.25]
    )
    return [float(v) for v in fit.convert(kind=np.polynomial.Polynomial).coef]


def monic_cubic(coeffs):
    scale = coeffs[3]
    low, mid, high = (c / scale for c in coeffs[:3])
    return scale, high, mid, low - high * mid


COS_SCALE, COS_A, COS_B, COS_C = monic_cubic(
    even_coeffs(lambda r: np.sqrt(2.0) * np.cos(np.pi * r), 3)
)
SIN_SCALE, SIN_A, SIN_B, SIN_C = monic_cubic(
    even_coeffs(lambda r: np.sqrt(2.0) * np.sin(np.pi * r) / r, 3)
)


def dft_tables(frames):
    turns = np.outer(np.arange(frames), np.arange(frames)) % (2 * frames)
    angle = turns * (np.pi / frames)
    sine = np.sin(angle)
    sine[:, 0] = 1.0 - 2.0 * (np.arange(frames) % 2)
    table = np.concatenate([np.cos(angle), sine], 1).astype(np.float32)
    high = table.astype(ml_dtypes.bfloat16)
    low = (table - high.astype(np.float32)).astype(ml_dtypes.bfloat16)
    return np.concatenate([high, high, low], 0), np.concatenate([high.T, low.T], 1)


def split(value):
    high = value.astype(jnp.bfloat16)
    low = (value - high.astype(jnp.float32)).astype(jnp.bfloat16)
    return high, low


def dot_rows(left, right):
    return lax.dot_general(
        left, right, (((1,), (1,)), ((), ())), preferred_element_type=jnp.float32
    )


def fused_kernel(
    tm_size,
    pos_hbm,
    vel_hbm,
    species_hbm,
    wave_hbm,
    table_hbm,
    back_hbm,
    out_ref,
    pos_ref,
    vel_ref,
    species_ref,
    wave_ref,
    table,
    back,
    wave_mat,
    coords,
    places,
    kinds,
    turns,
    acc,
    modes,
    from_pair,
    summed,
    signals,
    result,
    result_in,
    load_sem,
    pair_send,
    pair_recv,
    peer_send,
    peer_recv,
    last_send,
    last_recv,
):
    me = lax.axis_index("tm")
    core = lax.axis_index("atom")
    other = 1 - core
    frames = pos_ref.shape[1]
    waves = wave_ref.shape[1]
    atoms = pos_ref.shape[2]
    groups = frames // GROUP
    frame_total = frames * tm_size
    part = tm_size // 2
    units = frames // 2

    loads = [
        pltpu.make_async_copy(source, target, load_sem.at[n])
        for n, (source, target) in enumerate(
            (
                (wave_hbm, wave_ref),
                (species_hbm, species_ref),
                (vel_hbm, vel_ref),
                (pos_hbm, pos_ref),
                (table_hbm, table),
                (back_hbm, back),
            )
        )
    ]
    for load in loads:
        load.start()
    barrier = pltpu.get_barrier_semaphore()
    for hop in range(1, tm_size):
        peer = lax.rem(me + hop, tm_size)
        pl.semaphore_signal(
            barrier, inc=1, device_id=(peer, core), device_id_type=pl.DeviceIdType.MESH
        )
    pl.semaphore_signal(
        barrier, inc=1, device_id=(me, other), device_id_type=pl.DeviceIdType.MESH
    )

    loads[0].wait()
    waves_f = wave_ref[...].astype(jnp.float32)
    eight = jnp.concatenate(
        [waves_f[d : d + 1] for d in (0, 0, 1, 1, 2, 2)] + [jnp.zeros((2, waves), jnp.float32)], 0
    )
    wave_mat[...] = jnp.zeros_like(wave_mat)
    none = jnp.zeros((8, 128), jnp.float32)
    for phase in range(2):
        mine = eight[:, phase * 128 : phase * 128 + 128]
        pair = jnp.concatenate(
            [jnp.concatenate([mine, none], 1), jnp.concatenate([none, mine], 1)], 0
        ).astype(jnp.bfloat16)
        for n in range(GROUP // 2):
            wave_mat[phase, n, n * 16 : n * 16 + 16] = pair
    for load in loads[1:4]:
        load.wait()

    def scatter(target, place, value):
        for n in range(2):
            target[n, pl.ds(place, frames, stride=8), :] = value[:, n * 128 : n * 128 + 128]

    for d in range(3):
        x = pos_ref[d]
        scatter(coords, 2 * d, (x >> 7).astype(jnp.float32) * (1.0 / 128.0))
        scatter(coords, 2 * d + 1, (x & 127).astype(jnp.float32) * (1.0 / 16384.0))
    for d in (6, 7):
        scatter(coords, d, jnp.zeros((frames, atoms), jnp.float32))
    species_b = species_ref[...].astype(jnp.float32)
    species_a = 1.0 - species_b
    for q in range(4):
        for n, spec in enumerate((species_a, species_b)):
            if q == 0:
                rows = jnp.broadcast_to(spec, (frames, atoms))
            else:
                rows = vel_ref[q - 1] * spec
            scatter(kinds, 2 * q + n, rows)

    def trig(turn):
        rest = turn - jnp.round(turn)
        z = rest * rest
        zz = z * z
        half_sin = rest * ((z + SIN_A) * (zz + SIN_B) + SIN_C)
        half_cos = (z + COS_A) * (zz + COS_B) + COS_C
        return half_sin * half_sin, half_sin * half_cos

    def pair_copy(phase):
        return pltpu.make_async_remote_copy(
            src_ref=modes.at[phase, other],
            dst_ref=from_pair.at[phase],
            send_sem=pair_send.at[phase],
            recv_sem=pair_recv.at[phase],
            device_id=(me, other),
            device_id_type=pl.DeviceIdType.MESH,
        )

    def peer_copy(phase, hop):
        local = lax.rem(me + hop, part)
        return pltpu.make_async_remote_copy(
            src_ref=summed.at[phase, local],
            dst_ref=signals.at[me],
            send_sem=peer_send.at[phase, hop],
            recv_sem=peer_recv.at[me],
            device_id=(phase * part + local, core),
            device_id_type=pl.DeviceIdType.MESH,
        )

    def arrival(hop):
        peer = lax.rem(me + hop, tm_size)
        return pltpu.make_async_remote_copy(
            src_ref=summed.at[0, 0],
            dst_ref=signals.at[peer],
            send_sem=peer_send.at[0, 0],
            recv_sem=peer_recv.at[peer],
            device_id=(peer, core),
            device_id_type=pl.DeviceIdType.MESH,
        )

    def reduce_and_send(phase):
        pair_copy(phase).wait_recv()
        summed[phase] = modes[phase, core] + from_pair[phase]
        for hop in range(1, part):
            peer_copy(phase, hop).start()

        @pl.when(me // part == phase)
        def _():
            signals[me] = summed[phase, lax.rem(me, part)]

        @pl.when(me // part != phase)
        def _():
            peer_copy(phase, 0).start()

    half = atoms // 2

    for tg in range(groups):
        for n in range(2):
            block = coords[n, tg * GROUP * 8 : (tg + 1) * GROUP * 8, :]
            places[tg, n * 128 : n * 128 + 128] = block.T.astype(jnp.bfloat16)

    def find_turn(phase, unit, slot):
        turns[slot] = jnp.dot(
            places[unit // (GROUP // 2)],
            wave_mat[phase, unit % (GROUP // 2)],
            preferred_element_type=jnp.float32,
        )

    def one_unit(unit, slot):
        lefts, totals = [], []
        for k in range(2):
            rows = pl.ds(pl.multiple_of(unit * 16 + k * 8, 8), 8)
            kind = jnp.concatenate([kinds[0, rows, :], kinds[1, rows, :]], 1)
            totals.append(jnp.sum(kind, axis=1, keepdims=True))
            kind_high = kind.astype(jnp.bfloat16).astype(jnp.float32)
            lefts.append(jnp.concatenate([kind_high, kind - kind_high], 0).astype(jnp.bfloat16))
        sums = [None, None]
        for n in range(2):
            drop, sine = trig(turns[slot, n * half : n * half + half])
            for k in range(2):
                left = lefts[k][:, n * half : n * half + half]
                both = jnp.concatenate(
                    [v[:, k * 128 : k * 128 + 128] for v in (drop, sine)], 1
                )
                product = jnp.dot(
                    jnp.concatenate([left, left], 1),
                    jnp.concatenate(split(both), 0),
                    preferred_element_type=jnp.float32,
                )
                sums[k] = product if n == 0 else sums[k] + product
        for k in range(2):
            rows = pl.ds(pl.multiple_of(unit * 16 + k * 8, 8), 8)
            both = sums[k][:8] + sums[k][8:]
            acc[0, rows, :] = totals[k] - (SIN_SCALE * SIN_SCALE) * both[:, :128]
            acc[1, rows, :] = (SIN_SCALE * COS_SCALE) * both[:, 128:]

    def one_phase(phase, carry):
        find_turn(phase, 0, 0)

        def step(index, carry):
            @pl.when(jnp.logical_and(phase == 1, index == 0))
            def _():
                pl.semaphore_wait(barrier, tm_size)
                pair_copy(0).start()

            @pl.when(jnp.logical_and(phase == 1, index == SEND_STEP))
            def _():
                reduce_and_send(0)

            for k in range(STEP):
                unit = index * STEP + k
                find_turn(phase, jnp.minimum(unit + 1, units - 1), (k + 1) % 2)
                one_unit(unit, k % 2)
            return carry

        lax.fori_loop(0, units // STEP, step, 0)
        factors = wave_ref[:, pl.ds(pl.multiple_of(phase * 128, 128), 128)].astype(
            jnp.float32
        ) * (1.0 / WAVE_MAX)
        for tg in range(groups):
            rows = []
            for c in range(2):
                parts = [
                    acc[c, pl.ds(tg * GROUP * 8 + n, GROUP, stride=8), :] for n in range(8)
                ]
                rows += parts[:2]
                for n in range(2):
                    rows.append(
                        factors[0:1] * parts[2 + n]
                        + factors[1:2] * parts[4 + n]
                        + factors[2:3] * parts[6 + n]
                    )
            packed = jnp.concatenate(rows, 0).T.reshape(part, 2, 8, 128)
            modes[phase, 0, :, tg] = packed[:, 0]
            modes[phase, 1, :, tg] = packed[:, 1]

        @pl.when(phase == 1)
        def _():
            pair_copy(1).start()

        return carry

    lax.fori_loop(0, 2, one_phase, 0)
    reduce_and_send(1)
    for load in loads[4:]:
        load.wait()
    for hop in range(1, tm_size):
        arrival(hop).wait_recv()

    tiles = signals[...].reshape(frame_total // 128, 8, 8, 128)
    wide = frame_total // 128 * 8
    group_lane = lax.broadcasted_iota(jnp.int32, (wide, 128), 1) // 16
    turned = [
        pltpu.roll(tiles[:, p].reshape(wide, 128), 16 * p, 1) if p else tiles[:, p].reshape(wide, 128)
        for p in range(8)
    ]
    rows = []
    for m in range(8):
        picked = turned[0]
        for p in range(1, 8):
            picked = jnp.where(group_lane == (m + p) % 8, turned[p], picked)
        if m:
            picked = pltpu.roll(picked, 128 - 16 * m, 1)
        rows.append(
            jnp.concatenate([picked[v * 8 : v * 8 + 8] for v in range(frame_total // 128)], 1)
        )
    signal = jnp.concatenate(rows, 0)
    blocks = frame_total // BLOCK
    high, low = split(
        jnp.concatenate([signal[:, n * BLOCK : n * BLOCK + BLOCK] for n in range(blocks)], 0)
    )
    spectra = jnp.dot(
        jnp.concatenate([high, low, high], 1), table[...], preferred_element_type=jnp.float32
    )
    lane = lax.broadcasted_iota(jnp.int32, (8, BLOCK), 1)
    first = lane == 0
    flip = jnp.where(lane % 2 == 0, 1.0, -1.0)

    def spectrum(block, c, g, spec):
        row = block * 64 + (c * 4 + g * 2 + spec) * 8
        return spectra[row : row + 8, :BLOCK], spectra[row : row + 8, BLOCK:]

    out_rows = [[], []]
    for g in range(2):
        for a, b in ((0, 0), (0, 1), (1, 1)):
            shifts = []
            for shift in range(3):
                even = odd = imag = None
                for c in range(2):
                    for n in range(blocks - shift):
                        cos_a, sin_a = spectrum(n + shift, c, g, a)
                        cos_b, sin_b = spectrum(n, c, g, b)
                        terms = (cos_a * cos_b, sin_a * sin_b, sin_a * cos_b - cos_a * sin_b)
                        if even is None:
                            even, odd, imag = terms
                        else:
                            even, odd, imag = even + terms[0], odd + terms[1], imag + terms[2]
                shifts.append(
                    (
                        jnp.where(first, even, 2.0 * (even + odd)),
                        jnp.where(first, odd, 2.0 * imag),
                    )
                )
            for n in range(2):
                out_rows[n].append(
                    jnp.concatenate(
                        [now + flip * later for now, later in zip(shifts[n], shifts[n + 1])], 1
                    )
                )
    high, low = split(jnp.concatenate(out_rows[0] + out_rows[1], 0))
    both = jnp.dot(
        jnp.concatenate([high, low], 0), back[...], preferred_element_type=jnp.float32
    )
    corr = both[:96, :BLOCK] + both[96:, :BLOCK] + both[:96, BLOCK:]
    lag = lax.broadcasted_iota(jnp.int32, (1, BLOCK), 1)
    for n in range(2):
        norm = 1.0 / (
            (frame_total - n * BLOCK - lag).astype(jnp.float32)
            * jnp.float32(2 * BLOCK * 2 * atoms)
        )
        result[n] = (corr[n * 48 : n * 48 + 48] * norm).reshape(6, 8, BLOCK)
    swap = pltpu.make_async_remote_copy(
        src_ref=result.at[other],
        dst_ref=result_in,
        send_sem=last_send,
        recv_sem=last_recv,
        device_id=(me, other),
        device_id_type=pl.DeviceIdType.MESH,
    )
    swap.start()
    out_ref[:, pl.ds(pl.multiple_of(core * 8, 8), 8), :] = result[core]
    for phase in range(2):
        pair_copy(phase).wait_send()
        for hop in range(1, part):
            peer_copy(phase, hop).wait_send()

        @pl.when(me // part != phase)
        def _():
            peer_copy(phase, 0).wait_send()

    swap.wait()
    out_ref[:, pl.ds(pl.multiple_of(other * 8, 8), 8), :] = result_in[...]


def per_device_fused(tm_size, positions, velocities, species, wave_vectors):
    frames, atoms = positions.shape[1:]
    waves = wave_vectors.shape[1]
    groups = frames // GROUP
    frame_total = frames * tm_size
    lag_here = frame_total // 4
    vmem = pl.BlockSpec(memory_space=pltpu.VMEM)
    dma = pltpu.SemaphoreType.DMA
    return pl.pallas_call(
        lambda *refs: fused_kernel(tm_size, *refs),
        name="scattering",
        out_shape=jax.ShapeDtypeStruct((6, 16, lag_here), jnp.float32),
        in_specs=[pl.BlockSpec(memory_space=pltpu.HBM)] * 6,
        out_specs=vmem,
        scratch_shapes=[
            pltpu.VMEM(positions.shape, jnp.int32),
            pltpu.VMEM(velocities.shape, jnp.float32),
            pltpu.VMEM((1, atoms), jnp.int32),
            pltpu.VMEM(wave_vectors.shape, jnp.int32),
            pltpu.VMEM((3 * BLOCK, 2 * BLOCK), jnp.bfloat16),
            pltpu.VMEM((2 * BLOCK, 2 * BLOCK), jnp.bfloat16),
            pltpu.VMEM((2, GROUP // 2, 8 * GROUP, waves), jnp.bfloat16),
            pltpu.VMEM((2, 8 * frames, 128), jnp.float32),
            pltpu.VMEM((groups, atoms, 8 * GROUP), jnp.bfloat16),
            pltpu.VMEM((2, 8 * frames, 128), jnp.float32),
            pltpu.VMEM((2, atoms, waves), jnp.float32),
            pltpu.VMEM((2, 8 * frames, 128), jnp.float32),
            pltpu.VMEM((2, 2, tm_size // 2, groups, 8, 128), jnp.float32),
            pltpu.VMEM((2, tm_size // 2, groups, 8, 128), jnp.float32),
            pltpu.VMEM((2, tm_size // 2, groups, 8, 128), jnp.float32),
            pltpu.VMEM((tm_size, groups, 8, 128), jnp.float32),
            pltpu.VMEM((2, 6, 8, lag_here), jnp.float32),
            pltpu.VMEM((6, 8, lag_here), jnp.float32),
            dma((6,)),
            dma((2,)),
            dma((2,)),
            dma((2, tm_size // 2)),
            dma((tm_size,)),
            dma,
            dma,
        ],
        compiler_params=pltpu.CompilerParams(
            collective_id=0, has_side_effects=True, vmem_limit_bytes=48 << 20
        ),
    )(
        *(
            pltpu.with_memory_space_constraint(operand, pltpu.HBM)
            for operand in (
                positions,
                velocities,
                species.reshape(1, atoms),
                wave_vectors,
                *(jnp.asarray(table) for table in dft_tables(BLOCK)),
            )
        )
    )


def solution(mesh):
    tm_size = mesh.shape["tm"]
    atom_size = mesh.shape["atom"]

    def per_device(positions, velocities, species, wave_vectors):
        frames, atoms = positions.shape[1:]
        waves = wave_vectors.shape[1]
        fits = (
            tm_size == 16
            and atom_size == 2
            and frames == 2 * GROUP
            and atoms == 256
            and waves == 256
        )
        if fits:
            return per_device_fused(tm_size, positions, velocities, species, wave_vectors)
        return per_device_general(positions, velocities, species, wave_vectors)

    return jax.shard_map(
        per_device,
        mesh=mesh,
        in_specs=(P(None, "tm", "atom"), P(None, "tm", "atom"), P("atom"), P()),
        out_specs=P(None, "tm", "atom"),
        check_vma=False,
    )
```

```python
import math

import jax
import jax.numpy as jnp
import ml_dtypes
import numpy as np
from jax import lax
from jax.experimental import pallas as pl
from jax.experimental.pallas import tpu as pltpu
from jax.sharding import PartitionSpec as P

WAVE_MAX = 64


highest = lax.Precision.HIGHEST


def frame_block(pos_block, vel_block, species_onehot, wave_vectors):
    summed = (
        pos_block[0][:, :, None] * wave_vectors[0]
        + pos_block[1][:, :, None] * wave_vectors[1]
        + pos_block[2][:, :, None] * wave_vectors[2]
    )
    angle_unit = jnp.float32(2.0 * math.pi / 16384.0)
    phase = jnp.remainder(summed, 16384).astype(jnp.float32) * angle_unit
    kinds = jnp.concatenate([jnp.ones_like(vel_block[:1]), vel_block], 0)
    weights = kinds[:, None] * species_onehot[None, :, None, :]
    cos_part = jnp.einsum("qsba,bak->qsbk", weights, jnp.cos(phase), precision=highest)
    sin_part = jnp.einsum("qsba,bak->qsbk", weights, jnp.sin(phase), precision=highest)
    return jnp.stack([cos_part, sin_part])


def pair_terms(cos_rows, sin_rows):
    cos_a = cos_rows[:, :, 0]
    cos_b = cos_rows[:, :, 1]
    sin_a = sin_rows[:, :, 0]
    sin_b = sin_rows[:, :, 1]
    real_part = jnp.stack(
        [
            cos_a * cos_a + sin_a * sin_a,
            cos_a * cos_b + sin_a * sin_b,
            cos_b * cos_b + sin_b * sin_b,
        ],
        2,
    ).sum(0)
    imag_part = jnp.stack(
        [
            cos_a * sin_a - sin_a * cos_a,
            cos_a * sin_b - sin_a * cos_b,
            cos_b * sin_b - sin_b * cos_b,
        ],
        2,
    ).sum(0)
    return (real_part, imag_part)


def correlate(signals, atom_total):
    frame_total = signals.shape[-1]
    waves_here = signals.shape[3]
    signal_rows = signals.reshape(-1, frame_total)
    groups = lax.axis_size("atom")
    freq_count = frame_total // groups
    lag_count = frame_total // 2 // groups
    my_index = lax.axis_index("atom")
    freq_index = my_index * freq_count + jnp.arange(freq_count, dtype=jnp.int32)
    time_index = jnp.arange(frame_total, dtype=jnp.int32)
    angle_step = jnp.float32(math.pi / frame_total)
    turns = jnp.remainder(time_index[:, None] * freq_index[None, :], 2 * frame_total)
    angles = turns.astype(jnp.float32) * angle_step
    spec_cos = jnp.dot(signal_rows, jnp.cos(angles), precision=highest).reshape(
        2, 2, 2, waves_here, freq_count
    )
    spec_sin = jnp.dot(signal_rows, jnp.sin(angles), precision=highest).reshape(
        2, 2, 2, waves_here, freq_count
    )
    real_part, imag_part = pair_terms(spec_cos, spec_sin)
    spectral_weight = jnp.where(freq_index == 0, 1.0, 2.0).astype(jnp.float32)
    real_rows = (real_part * spectral_weight).reshape(6 * waves_here, freq_count)
    imag_rows = (imag_part * spectral_weight).reshape(6 * waves_here, freq_count)
    alternating = jnp.where(time_index % 2 == 0, 1.0, -1.0).astype(jnp.float32)
    nyquist = jnp.dot(signal_rows, alternating, precision=highest).reshape(2, 2, 2, waves_here)
    nyq_a = nyquist[:, :, 0]
    nyq_b = nyquist[:, :, 1]
    nyq_real = (
        jnp.stack([nyq_a * nyq_a, nyq_a * nyq_b, nyq_b * nyq_b], 2).sum(0).reshape(6 * waves_here)
    )
    nyq_here = nyq_real * jnp.where(my_index == 0, 1.0, 0.0).astype(jnp.float32)
    lag_index = jnp.arange(lag_count * lax.axis_size("atom"), dtype=jnp.int32)
    lag_turns = jnp.remainder(lag_index[:, None] * freq_index[None, :], 2 * frame_total)
    lag_angles = lag_turns.astype(jnp.float32) * angle_step
    term = jnp.dot(jnp.cos(lag_angles), real_rows.T, precision=highest) - jnp.dot(
        jnp.sin(lag_angles), imag_rows.T, precision=highest
    )
    lag_sign = jnp.where(lag_index % 2 == 0, 1.0, -1.0).astype(jnp.float32)
    shared = lax.psum_scatter(
        term + lag_sign[:, None] * nyq_here[None, :], "atom", scatter_dimension=0, tiled=True
    )
    lag_index = my_index * lag_count + jnp.arange(lag_count, dtype=jnp.int32)
    scaled = shared / jnp.float32(2 * frame_total)
    isf = (
        scaled / (jnp.float32(atom_total) * (frame_total - lag_index).astype(jnp.float32))[:, None]
    )
    return isf.T.reshape(6, waves_here, lag_count)


def per_device_general(positions, velocities, species, wave_vectors):
    atom_count = positions.shape[2]
    frame_count = positions.shape[1]
    wave_count = wave_vectors.shape[1]
    block_size = math.gcd(frame_count, 2)
    block_count = frame_count // block_size
    species_onehot = jnp.stack([1 - species, species]).astype(jnp.float32)
    pos_blocks = positions.reshape(3, block_count, block_size, atom_count).transpose(1, 0, 2, 3)
    vel_blocks = velocities.reshape(3, block_count, block_size, atom_count).transpose(1, 0, 2, 3)
    raw_modes = lax.map(
        lambda operands: frame_block(operands[0], operands[1], species_onehot, wave_vectors),
        (pos_blocks, vel_blocks),
    )
    raw_modes = raw_modes.transpose(1, 2, 3, 0, 4, 5).reshape(2, 4, 2, frame_count, wave_count)
    wave_scaled = wave_vectors.astype(jnp.float32) / WAVE_MAX
    current = (
        wave_scaled[0] * raw_modes[:, 1]
        + wave_scaled[1] * raw_modes[:, 2]
        + wave_scaled[2] * raw_modes[:, 3]
    )
    modes = jnp.stack([raw_modes[:, 0], current], 1)
    atom_groups = lax.axis_size("atom")
    summed = lax.psum(modes, "atom")
    owned = lax.all_to_all(summed, "tm", split_axis=4, concat_axis=3, tiled=True)
    signals = jnp.moveaxis(owned, 3, 4)
    return correlate(signals, atom_count * atom_groups)


GROUP = 16
STEP = 4
BLOCK = 128
PHASES = 4


def even_coeffs(func, degree):
    fit = np.polynomial.chebyshev.Chebyshev.interpolate(
        lambda z: func(np.sqrt(np.maximum(z, 1e-12))), degree, domain=[0.0, 0.25]
    )
    return [float(v) for v in fit.convert(kind=np.polynomial.Polynomial).coef]


def monic_cubic(coeffs):
    scale = coeffs[3]
    low, mid, high = (c / scale for c in coeffs[:3])
    return scale, high, mid, low - high * mid


COS_SCALE, COS_A, COS_B, COS_C = monic_cubic(
    even_coeffs(lambda r: np.sqrt(2.0) * np.cos(np.pi * r), 3)
)
SIN_SCALE, SIN_A, SIN_B, SIN_C = monic_cubic(
    even_coeffs(lambda r: np.sqrt(2.0) * np.sin(np.pi * r) / r, 3)
)


def dft_tables(frames):
    turns = np.outer(np.arange(frames), np.arange(frames)) % (2 * frames)
    angle = turns * (np.pi / frames)
    sine = np.sin(angle)
    sine[:, 0] = 1.0 - 2.0 * (np.arange(frames) % 2)
    table = np.concatenate([np.cos(angle), sine], 1).astype(np.float32)
    high = table.astype(ml_dtypes.bfloat16)
    low = (table - high.astype(np.float32)).astype(ml_dtypes.bfloat16)
    return np.concatenate([high, high, low], 0), np.concatenate([high.T, low.T], 1)


def split(value):
    high = value.astype(jnp.bfloat16)
    low = (value - high.astype(jnp.float32)).astype(jnp.bfloat16)
    return high, low


def dot_rows(left, right):
    return lax.dot_general(
        left, right, (((1,), (1,)), ((), ())), preferred_element_type=jnp.float32
    )


def trade(slot):
    return jnp.where(slot == 11, 12, jnp.where(slot == 12, 11, slot))


def fused_kernel(
    tm_size,
    pos_hbm,
    vel_hbm,
    species_hbm,
    wave_hbm,
    table_hbm,
    back_hbm,
    out_ref,
    pos_ref,
    vel_ref,
    species_ref,
    wave_ref,
    table,
    back,
    wave_mat,
    coords,
    places,
    factor,
    kinds,
    turns,
    acc,
    modes,
    from_pair,
    summed,
    signals,
    result,
    result_in,
    load_sem,
    pair_send,
    pair_recv,
    peer_send,
    peer_recv,
    last_send,
    last_recv,
):
    me = lax.axis_index("tm")
    core = lax.axis_index("atom")
    other = 1 - core
    frames = pos_ref.shape[1]
    waves = wave_ref.shape[1]
    atoms = pos_ref.shape[2]
    groups = frames // GROUP
    frame_total = frames * tm_size
    part = tm_size // PHASES
    place = trade(me)
    units = frames // 4
    steps = units // STEP

    loads = [
        pltpu.make_async_copy(source, target, load_sem.at[n])
        for n, (source, target) in enumerate(
            (
                (wave_hbm, wave_ref),
                (species_hbm, species_ref),
                (vel_hbm, vel_ref),
                (pos_hbm, pos_ref),
                (table_hbm, table),
                (back_hbm, back),
            )
        )
    ]
    for load in loads:
        load.start()
    barrier = pltpu.get_barrier_semaphore()
    for hop in range(1, tm_size):
        peer = lax.rem(me + hop, tm_size)
        pl.semaphore_signal(
            barrier, inc=1, device_id=(peer, core), device_id_type=pl.DeviceIdType.MESH
        )
    pl.semaphore_signal(
        barrier, inc=1, device_id=(me, other), device_id_type=pl.DeviceIdType.MESH
    )

    loads[0].wait()
    waves_f = wave_ref[...].astype(jnp.float32)
    eight = jnp.concatenate(
        [waves_f[d : d + 1] for d in (0, 0, 1, 1, 2, 2)] + [jnp.zeros((2, waves), jnp.float32)], 0
    )
    wave_mat[...] = jnp.zeros_like(wave_mat)
    none = jnp.zeros((8, 128), jnp.float32)
    lane_group = lax.broadcasted_iota(jnp.int32, (8, 128), 1) // 16
    low_lane = lane_group < 4
    for phase in range(PHASES):
        tile = eight[:, phase // 2 * 128 : phase // 2 * 128 + 128]
        if phase >= 2:
            tile = jnp.where(
                lane_group == 3,
                pltpu.roll(tile, 112, 1),
                jnp.where(lane_group == 4, pltpu.roll(tile, 16, 1), tile),
            )
        turned = pltpu.roll(tile, 64, 1)
        twice = jnp.where(low_lane, turned, tile) if phase % 2 else jnp.where(low_lane, tile, turned)
        factor[phase] = twice * (1.0 / WAVE_MAX)
        for b, mine in enumerate((jnp.where(low_lane, twice, 0.0), jnp.where(low_lane, 0.0, twice))):
            pair = jnp.concatenate(
                [jnp.concatenate([mine, none], 1), jnp.concatenate([none, mine], 1)], 0
            ).astype(jnp.bfloat16)
            for n in range(4):
                row = b * 64 + n * 16
                wave_mat[phase, n, row : row + 16] = pair
    for load in loads[1:4]:
        load.wait()

    def scatter(target, place, value):
        for n in range(2):
            target[n, pl.ds(place, frames, stride=8), :] = value[:, n * 128 : n * 128 + 128]

    for d in range(3):
        x = pos_ref[d]
        scatter(coords, 2 * d, (x >> 7).astype(jnp.float32) * (1.0 / 128.0))
        scatter(coords, 2 * d + 1, (x & 127).astype(jnp.float32) * (1.0 / 16384.0))
    for d in (6, 7):
        scatter(coords, d, jnp.zeros((frames, atoms), jnp.float32))
    species_b = species_ref[...].astype(jnp.float32)
    species_a = 1.0 - species_b
    for q in range(4):
        for n, spec in enumerate((species_a, species_b)):
            if q == 0:
                rows = jnp.broadcast_to(spec, (frames, atoms))
            else:
                rows = vel_ref[q - 1] * spec
            scatter(kinds, 2 * q + n, rows)

    def trig(turn):
        rest = turn - jnp.round(turn)
        z = rest * rest
        zz = z * z
        half_sin = rest * ((z + SIN_A) * (zz + SIN_B) + SIN_C)
        half_cos = (z + COS_A) * (zz + COS_B) + COS_C
        return half_sin * half_sin, half_sin * half_cos

    def pair_copy(phase):
        return pltpu.make_async_remote_copy(
            src_ref=modes.at[phase, other],
            dst_ref=from_pair.at[phase],
            send_sem=pair_send.at[phase],
            recv_sem=pair_recv.at[phase],
            device_id=(me, other),
            device_id_type=pl.DeviceIdType.MESH,
        )

    def peer_copy(phase, hop):
        local = lax.rem(place + hop, part)
        return pltpu.make_async_remote_copy(
            src_ref=summed.at[phase, local],
            dst_ref=signals.at[me],
            send_sem=peer_send.at[phase, hop],
            recv_sem=peer_recv.at[me],
            device_id=(trade(phase * part + local), core),
            device_id_type=pl.DeviceIdType.MESH,
        )

    def arrival(hop):
        peer = lax.rem(me + hop, tm_size)
        return pltpu.make_async_remote_copy(
            src_ref=summed.at[0, 0],
            dst_ref=signals.at[peer],
            send_sem=peer_send.at[0, 0],
            recv_sem=peer_recv.at[peer],
            device_id=(peer, core),
            device_id_type=pl.DeviceIdType.MESH,
        )

    def reduce_and_send(phase):
        pair_copy(phase).wait_recv()
        summed[phase] = modes[phase, core] + from_pair[phase]
        for hop in range(1, part):
            peer_copy(phase, hop).start()

        @pl.when(place // part == phase)
        def _():
            signals[me] = summed[phase, lax.rem(place, part)]

        @pl.when(place // part != phase)
        def _():
            peer_copy(phase, 0).start()

    half = atoms // 2

    for tg in range(groups):
        for n in range(2):
            block = jnp.concatenate(
                [coords[n, m * 128 + tg * 64 : m * 128 + tg * 64 + 64, :] for m in range(2)], 0
            )
            places[tg, n * 128 : n * 128 + 128] = block.T.astype(jnp.bfloat16)

    def find_turn(phase, unit, slot):
        turns[slot] = jnp.dot(
            places[unit // 4],
            wave_mat[phase, unit % 4],
            preferred_element_type=jnp.float32,
        )

    def one_unit(unit, slot):
        lefts, totals = [], []
        for k in range(2):
            stack = []
            for m in range(2):
                rows = pl.ds(pl.multiple_of(unit * 16 + m * 128 + k * 8, 8), 8)
                kind = jnp.concatenate([kinds[0, rows, :], kinds[1, rows, :]], 1)
                totals.append(jnp.sum(kind, axis=1, keepdims=True))
                kind_high = kind.astype(jnp.bfloat16).astype(jnp.float32)
                stack += [kind_high, kind - kind_high]
            lefts.append(jnp.concatenate(stack, 0).astype(jnp.bfloat16))
        sums = [None, None]
        for n in range(2):
            drop, sine = trig(turns[slot, n * half : n * half + half])
            for k in range(2):
                left = lefts[k][:, n * half : n * half + half]
                both = jnp.concatenate(
                    [v[:, k * 128 : k * 128 + 128] for v in (drop, sine)], 1
                )
                product = jnp.dot(
                    jnp.concatenate([left, left], 1),
                    jnp.concatenate(split(both), 0),
                    preferred_element_type=jnp.float32,
                )
                sums[k] = product if n == 0 else sums[k] + product
        for k in range(2):
            rows = pl.ds(pl.multiple_of(unit * 16 + k * 8, 8), 8)
            here = sums[k][:8] + sums[k][8:16]
            later = sums[k][16:24] + sums[k][24:]
            total = jnp.where(low_lane, totals[2 * k], totals[2 * k + 1])
            drop = jnp.where(low_lane, here[:, :128], later[:, :128])
            sine = jnp.where(low_lane, here[:, 128:], later[:, 128:])
            acc[0, rows, :] = total - (SIN_SCALE * SIN_SCALE) * drop
            acc[1, rows, :] = (SIN_SCALE * COS_SCALE) * sine

    def one_phase(phase, carry):
        find_turn(phase, 0, 0)

        def step(index, carry):
            @pl.when(jnp.logical_and(phase == 1, index == steps - 1))
            def _():
                pl.semaphore_wait(barrier, tm_size)
                pair_copy(0).start()

            @pl.when(jnp.logical_and(phase == 2, index == 0))
            def _():
                reduce_and_send(0)

            @pl.when(jnp.logical_and(phase >= 2, index == steps - 1))
            def _():
                reduce_and_send(phase - 1)

            for k in range(STEP):
                unit = index * STEP + k
                find_turn(phase, jnp.minimum(unit + 1, units - 1), (k + 1) % 2)
                one_unit(unit, k % 2)
            return carry

        lax.fori_loop(0, steps, step, 0)
        rows = []
        for c in range(2):
            parts = [acc[c, pl.ds(n, GROUP, stride=8), :] for n in range(8)]
            rows += parts[:2]
            for n in range(2):
                rows.append(
                    factor[phase, 0:1] * parts[2 + n]
                    + factor[phase, 2:3] * parts[4 + n]
                    + factor[phase, 4:5] * parts[6 + n]
                )
        packed = jnp.concatenate(rows, 0).T.reshape(2, part, 2, 8, 128)
        for n in range(2):
            for m in range(2):
                modes[phase, n, :, m] = packed[m, :, n]

        @pl.when(phase >= 1)
        def _():
            pair_copy(phase).start()

        return carry

    lax.fori_loop(0, PHASES, one_phase, 0)
    reduce_and_send(PHASES - 1)
    for load in loads[4:]:
        load.wait()
    for hop in range(1, tm_size):
        arrival(hop).wait_recv()

    tiles = signals[...].reshape(frame_total // 128, 8, 8, 128)
    wide = frame_total // 128 * 8
    group_lane = lax.broadcasted_iota(jnp.int32, (wide, 128), 1) // 16
    turned = [
        pltpu.roll(tiles[:, p].reshape(wide, 128), 16 * p, 1) if p else tiles[:, p].reshape(wide, 128)
        for p in range(8)
    ]
    rows = []
    for m in range(8):
        picked = turned[0]
        for p in range(1, 8):
            picked = jnp.where(group_lane == (m + p) % 8, turned[p], picked)
        if m:
            picked = pltpu.roll(picked, 128 - 16 * m, 1)
        rows.append(
            jnp.concatenate([picked[v * 8 : v * 8 + 8] for v in range(frame_total // 128)], 1)
        )
    signal = jnp.concatenate(rows, 0)
    blocks = frame_total // BLOCK
    high, low = split(
        jnp.concatenate([signal[:, n * BLOCK : n * BLOCK + BLOCK] for n in range(blocks)], 0)
    )
    spectra = jnp.dot(
        jnp.concatenate([high, low, high], 1), table[...], preferred_element_type=jnp.float32
    )
    lane = lax.broadcasted_iota(jnp.int32, (8, BLOCK), 1)
    first = lane == 0
    flip = jnp.where(lane % 2 == 0, 1.0, -1.0)

    def spectrum(block, c, g, spec):
        row = block * 64 + (c * 4 + g * 2 + spec) * 8
        return spectra[row : row + 8, :BLOCK], spectra[row : row + 8, BLOCK:]

    out_rows = [[], []]
    for g in range(2):
        for a, b in ((0, 0), (0, 1), (1, 1)):
            shifts = []
            for shift in range(3):
                even = odd = imag = None
                for c in range(2):
                    for n in range(blocks - shift):
                        cos_a, sin_a = spectrum(n + shift, c, g, a)
                        cos_b, sin_b = spectrum(n, c, g, b)
                        terms = (cos_a * cos_b, sin_a * sin_b, sin_a * cos_b - cos_a * sin_b)
                        if even is None:
                            even, odd, imag = terms
                        else:
                            even, odd, imag = even + terms[0], odd + terms[1], imag + terms[2]
                shifts.append(
                    (
                        jnp.where(first, even, 2.0 * (even + odd)),
                        jnp.where(first, odd, 2.0 * imag),
                    )
                )
            for n in range(2):
                out_rows[n].append(
                    jnp.concatenate(
                        [now + flip * later for now, later in zip(shifts[n], shifts[n + 1])], 1
                    )
                )
    high, low = split(jnp.concatenate(out_rows[0] + out_rows[1], 0))
    both = jnp.dot(
        jnp.concatenate([high, low], 0), back[...], preferred_element_type=jnp.float32
    )
    corr = both[:96, :BLOCK] + both[96:, :BLOCK] + both[:96, BLOCK:]
    lag = lax.broadcasted_iota(jnp.int32, (1, BLOCK), 1)
    for n in range(2):
        norm = 1.0 / (
            (frame_total - n * BLOCK - lag).astype(jnp.float32)
            * jnp.float32(2 * BLOCK * 2 * atoms)
        )
        result[n] = (corr[n * 48 : n * 48 + 48] * norm).reshape(6, 8, BLOCK)
    swap = pltpu.make_async_remote_copy(
        src_ref=result.at[other],
        dst_ref=result_in,
        send_sem=last_send,
        recv_sem=last_recv,
        device_id=(me, other),
        device_id_type=pl.DeviceIdType.MESH,
    )
    swap.start()
    out_ref[:, pl.ds(pl.multiple_of(core * 8, 8), 8), :] = result[core]
    for phase in range(PHASES):
        pair_copy(phase).wait_send()
        for hop in range(1, part):
            peer_copy(phase, hop).wait_send()

        @pl.when(place // part != phase)
        def _():
            peer_copy(phase, 0).wait_send()

    swap.wait()
    out_ref[:, pl.ds(pl.multiple_of(other * 8, 8), 8), :] = result_in[...]


def per_device_fused(tm_size, positions, velocities, species, wave_vectors):
    frames, atoms = positions.shape[1:]
    waves = wave_vectors.shape[1]
    groups = frames // GROUP
    frame_total = frames * tm_size
    lag_here = frame_total // 4
    vmem = pl.BlockSpec(memory_space=pltpu.VMEM)
    dma = pltpu.SemaphoreType.DMA
    return pl.pallas_call(
        lambda *refs: fused_kernel(tm_size, *refs),
        name="scattering",
        out_shape=jax.ShapeDtypeStruct((6, 16, lag_here), jnp.float32),
        in_specs=[pl.BlockSpec(memory_space=pltpu.HBM)] * 6,
        out_specs=vmem,
        scratch_shapes=[
            pltpu.VMEM(positions.shape, jnp.int32),
            pltpu.VMEM(velocities.shape, jnp.float32),
            pltpu.VMEM((1, atoms), jnp.int32),
            pltpu.VMEM(wave_vectors.shape, jnp.int32),
            pltpu.VMEM((3 * BLOCK, 2 * BLOCK), jnp.bfloat16),
            pltpu.VMEM((2 * BLOCK, 2 * BLOCK), jnp.bfloat16),
            pltpu.VMEM((PHASES, 4, 8 * GROUP, waves), jnp.bfloat16),
            pltpu.VMEM((2, 8 * frames, 128), jnp.float32),
            pltpu.VMEM((groups, atoms, 8 * GROUP), jnp.bfloat16),
            pltpu.VMEM((PHASES, 8, 128), jnp.float32),
            pltpu.VMEM((2, 8 * frames, 128), jnp.float32),
            pltpu.VMEM((2, atoms, waves), jnp.float32),
            pltpu.VMEM((2, 8 * GROUP, 128), jnp.float32),
            pltpu.VMEM((PHASES, 2, tm_size // PHASES, groups, 8, 128), jnp.float32),
            pltpu.VMEM((PHASES, tm_size // PHASES, groups, 8, 128), jnp.float32),
            pltpu.VMEM((PHASES, tm_size // PHASES, groups, 8, 128), jnp.float32),
            pltpu.VMEM((tm_size, groups, 8, 128), jnp.float32),
            pltpu.VMEM((2, 6, 8, lag_here), jnp.float32),
            pltpu.VMEM((6, 8, lag_here), jnp.float32),
            dma((6,)),
            dma((PHASES,)),
            dma((PHASES,)),
            dma((PHASES, tm_size // PHASES)),
            dma((tm_size,)),
            dma,
            dma,
        ],
        compiler_params=pltpu.CompilerParams(
            collective_id=0, has_side_effects=True, vmem_limit_bytes=48 << 20
        ),
    )(
        *(
            pltpu.with_memory_space_constraint(operand, pltpu.HBM)
            for operand in (
                positions,
                velocities,
                species.reshape(1, atoms),
                wave_vectors,
                *(jnp.asarray(table) for table in dft_tables(BLOCK)),
            )
        )
    )


def solution(mesh):
    tm_size = mesh.shape["tm"]
    atom_size = mesh.shape["atom"]

    def per_device(positions, velocities, species, wave_vectors):
        frames, atoms = positions.shape[1:]
        waves = wave_vectors.shape[1]
        fits = (
            tm_size == 16
            and atom_size == 2
            and frames == 2 * GROUP
            and atoms == 256
            and waves == 256
        )
        if fits:
            return per_device_fused(tm_size, positions, velocities, species, wave_vectors)
        return per_device_general(positions, velocities, species, wave_vectors)

    return jax.shard_map(
        per_device,
        mesh=mesh,
        in_specs=(P(None, "tm", "atom"), P(None, "tm", "atom"), P("atom"), P()),
        out_specs=P(None, "tm", "atom"),
        check_vma=False,
    )
```

```python
import math

import jax
import jax.numpy as jnp
import ml_dtypes
import numpy as np
from jax import lax
from jax.experimental import pallas as pl
from jax.experimental.pallas import tpu as pltpu
from jax.sharding import PartitionSpec as P

WAVE_MAX = 64


highest = lax.Precision.HIGHEST


def frame_block(pos_block, vel_block, species_onehot, wave_vectors):
    summed = (
        pos_block[0][:, :, None] * wave_vectors[0]
        + pos_block[1][:, :, None] * wave_vectors[1]
        + pos_block[2][:, :, None] * wave_vectors[2]
    )
    angle_unit = jnp.float32(2.0 * math.pi / 16384.0)
    phase = jnp.remainder(summed, 16384).astype(jnp.float32) * angle_unit
    kinds = jnp.concatenate([jnp.ones_like(vel_block[:1]), vel_block], 0)
    weights = kinds[:, None] * species_onehot[None, :, None, :]
    cos_part = jnp.einsum("qsba,bak->qsbk", weights, jnp.cos(phase), precision=highest)
    sin_part = jnp.einsum("qsba,bak->qsbk", weights, jnp.sin(phase), precision=highest)
    return jnp.stack([cos_part, sin_part])


def pair_terms(cos_rows, sin_rows):
    cos_a = cos_rows[:, :, 0]
    cos_b = cos_rows[:, :, 1]
    sin_a = sin_rows[:, :, 0]
    sin_b = sin_rows[:, :, 1]
    real_part = jnp.stack(
        [
            cos_a * cos_a + sin_a * sin_a,
            cos_a * cos_b + sin_a * sin_b,
            cos_b * cos_b + sin_b * sin_b,
        ],
        2,
    ).sum(0)
    imag_part = jnp.stack(
        [
            cos_a * sin_a - sin_a * cos_a,
            cos_a * sin_b - sin_a * cos_b,
            cos_b * sin_b - sin_b * cos_b,
        ],
        2,
    ).sum(0)
    return (real_part, imag_part)


def correlate(signals, atom_total):
    frame_total = signals.shape[-1]
    waves_here = signals.shape[3]
    signal_rows = signals.reshape(-1, frame_total)
    groups = lax.axis_size("atom")
    freq_count = frame_total // groups
    lag_count = frame_total // 2 // groups
    my_index = lax.axis_index("atom")
    freq_index = my_index * freq_count + jnp.arange(freq_count, dtype=jnp.int32)
    time_index = jnp.arange(frame_total, dtype=jnp.int32)
    angle_step = jnp.float32(math.pi / frame_total)
    turns = jnp.remainder(time_index[:, None] * freq_index[None, :], 2 * frame_total)
    angles = turns.astype(jnp.float32) * angle_step
    spec_cos = jnp.dot(signal_rows, jnp.cos(angles), precision=highest).reshape(
        2, 2, 2, waves_here, freq_count
    )
    spec_sin = jnp.dot(signal_rows, jnp.sin(angles), precision=highest).reshape(
        2, 2, 2, waves_here, freq_count
    )
    real_part, imag_part = pair_terms(spec_cos, spec_sin)
    spectral_weight = jnp.where(freq_index == 0, 1.0, 2.0).astype(jnp.float32)
    real_rows = (real_part * spectral_weight).reshape(6 * waves_here, freq_count)
    imag_rows = (imag_part * spectral_weight).reshape(6 * waves_here, freq_count)
    alternating = jnp.where(time_index % 2 == 0, 1.0, -1.0).astype(jnp.float32)
    nyquist = jnp.dot(signal_rows, alternating, precision=highest).reshape(2, 2, 2, waves_here)
    nyq_a = nyquist[:, :, 0]
    nyq_b = nyquist[:, :, 1]
    nyq_real = (
        jnp.stack([nyq_a * nyq_a, nyq_a * nyq_b, nyq_b * nyq_b], 2).sum(0).reshape(6 * waves_here)
    )
    nyq_here = nyq_real * jnp.where(my_index == 0, 1.0, 0.0).astype(jnp.float32)
    lag_index = jnp.arange(lag_count * lax.axis_size("atom"), dtype=jnp.int32)
    lag_turns = jnp.remainder(lag_index[:, None] * freq_index[None, :], 2 * frame_total)
    lag_angles = lag_turns.astype(jnp.float32) * angle_step
    term = jnp.dot(jnp.cos(lag_angles), real_rows.T, precision=highest) - jnp.dot(
        jnp.sin(lag_angles), imag_rows.T, precision=highest
    )
    lag_sign = jnp.where(lag_index % 2 == 0, 1.0, -1.0).astype(jnp.float32)
    shared = lax.psum_scatter(
        term + lag_sign[:, None] * nyq_here[None, :], "atom", scatter_dimension=0, tiled=True
    )
    lag_index = my_index * lag_count + jnp.arange(lag_count, dtype=jnp.int32)
    scaled = shared / jnp.float32(2 * frame_total)
    isf = (
        scaled / (jnp.float32(atom_total) * (frame_total - lag_index).astype(jnp.float32))[:, None]
    )
    return isf.T.reshape(6, waves_here, lag_count)


def per_device_general(positions, velocities, species, wave_vectors):
    atom_count = positions.shape[2]
    frame_count = positions.shape[1]
    wave_count = wave_vectors.shape[1]
    block_size = math.gcd(frame_count, 2)
    block_count = frame_count // block_size
    species_onehot = jnp.stack([1 - species, species]).astype(jnp.float32)
    pos_blocks = positions.reshape(3, block_count, block_size, atom_count).transpose(1, 0, 2, 3)
    vel_blocks = velocities.reshape(3, block_count, block_size, atom_count).transpose(1, 0, 2, 3)
    raw_modes = lax.map(
        lambda operands: frame_block(operands[0], operands[1], species_onehot, wave_vectors),
        (pos_blocks, vel_blocks),
    )
    raw_modes = raw_modes.transpose(1, 2, 3, 0, 4, 5).reshape(2, 4, 2, frame_count, wave_count)
    wave_scaled = wave_vectors.astype(jnp.float32) / WAVE_MAX
    current = (
        wave_scaled[0] * raw_modes[:, 1]
        + wave_scaled[1] * raw_modes[:, 2]
        + wave_scaled[2] * raw_modes[:, 3]
    )
    modes = jnp.stack([raw_modes[:, 0], current], 1)
    atom_groups = lax.axis_size("atom")
    summed = lax.psum(modes, "atom")
    owned = lax.all_to_all(summed, "tm", split_axis=4, concat_axis=3, tiled=True)
    signals = jnp.moveaxis(owned, 3, 4)
    return correlate(signals, atom_count * atom_groups)


GROUP = 16
STEP = 4
BLOCK = 128
PHASES = 4


def even_coeffs(func, degree):
    fit = np.polynomial.chebyshev.Chebyshev.interpolate(
        lambda z: func(np.sqrt(np.maximum(z, 1e-12))), degree, domain=[0.0, 0.25]
    )
    return [float(v) for v in fit.convert(kind=np.polynomial.Polynomial).coef]


def monic_cubic(coeffs):
    scale = coeffs[3]
    low, mid, high = (c / scale for c in coeffs[:3])
    return scale, high, mid, low - high * mid


COS_SCALE, COS_A, COS_B, COS_C = monic_cubic(
    even_coeffs(lambda r: np.sqrt(2.0) * np.cos(np.pi * r), 3)
)
SIN_SCALE, SIN_A, SIN_B, SIN_C = monic_cubic(
    even_coeffs(lambda r: np.sqrt(2.0) * np.sin(np.pi * r) / r, 3)
)


def dft_tables(frames):
    turns = np.outer(np.arange(frames), np.arange(frames)) % (2 * frames)
    angle = turns * (np.pi / frames)
    sine = np.sin(angle)
    sine[:, 0] = 1.0 - 2.0 * (np.arange(frames) % 2)
    table = np.concatenate([np.cos(angle), sine], 1).astype(np.float32)
    high = table.astype(ml_dtypes.bfloat16)
    low = (table - high.astype(np.float32)).astype(ml_dtypes.bfloat16)
    return np.concatenate([high, high, low], 0), np.concatenate([high.T, low.T], 1)


def split(value):
    high = value.astype(jnp.bfloat16)
    low = (value - high.astype(jnp.float32)).astype(jnp.bfloat16)
    return high, low


def dot_rows(left, right):
    return lax.dot_general(
        left, right, (((1,), (1,)), ((), ())), preferred_element_type=jnp.float32
    )


def trade(slot):
    return jnp.where(slot == 11, 12, jnp.where(slot == 12, 11, slot))


def fused_kernel(
    tm_size,
    pos_hbm,
    vel_hbm,
    species_hbm,
    wave_hbm,
    table_hbm,
    back_hbm,
    out_ref,
    pos_ref,
    vel_ref,
    species_ref,
    wave_ref,
    table,
    back,
    wave_mat,
    coords,
    places,
    factor,
    kinds,
    turns,
    acc,
    modes,
    from_pair,
    summed,
    signals,
    result,
    result_in,
    load_sem,
    pair_send,
    pair_recv,
    peer_send,
    peer_recv,
    last_send,
    last_recv,
):
    me = lax.axis_index("tm")
    core = lax.axis_index("atom")
    other = 1 - core
    frames = pos_ref.shape[1]
    waves = wave_ref.shape[1]
    atoms = pos_ref.shape[2]
    groups = frames // GROUP
    frame_total = frames * tm_size
    part = tm_size // PHASES
    place = trade(me)
    units = frames // 4
    steps = units // STEP

    loads = [
        pltpu.make_async_copy(source, target, load_sem.at[n])
        for n, (source, target) in enumerate(
            (
                (wave_hbm, wave_ref),
                (species_hbm, species_ref),
                (vel_hbm, vel_ref),
                (pos_hbm, pos_ref),
                (table_hbm, table),
                (back_hbm, back),
            )
        )
    ]
    for load in loads:
        load.start()
    barrier = pltpu.get_barrier_semaphore()
    for hop in range(1, tm_size):
        peer = lax.rem(me + hop, tm_size)
        pl.semaphore_signal(
            barrier, inc=1, device_id=(peer, core), device_id_type=pl.DeviceIdType.MESH
        )
    pl.semaphore_signal(
        barrier, inc=1, device_id=(me, other), device_id_type=pl.DeviceIdType.MESH
    )

    loads[0].wait()
    waves_f = wave_ref[...].astype(jnp.float32)
    eight = jnp.concatenate(
        [waves_f[d : d + 1] for d in (0, 0, 1, 1, 2, 2)] + [jnp.zeros((2, waves), jnp.float32)], 0
    )
    wave_mat[...] = jnp.zeros_like(wave_mat)
    none = jnp.zeros((8, 128), jnp.float32)
    lane_group = lax.broadcasted_iota(jnp.int32, (8, 128), 1) // 16
    low_lane = lane_group < 4
    for phase in range(PHASES):
        tile = eight[:, phase // 2 * 128 : phase // 2 * 128 + 128]
        if phase >= 2:
            tile = jnp.where(
                lane_group == 3,
                pltpu.roll(tile, 112, 1),
                jnp.where(lane_group == 4, pltpu.roll(tile, 16, 1), tile),
            )
        turned = pltpu.roll(tile, 64, 1)
        twice = jnp.where(low_lane, turned, tile) if phase % 2 else jnp.where(low_lane, tile, turned)
        factor[phase] = twice * (1.0 / WAVE_MAX)
        for b, mine in enumerate((jnp.where(low_lane, twice, 0.0), jnp.where(low_lane, 0.0, twice))):
            pair = jnp.concatenate(
                [jnp.concatenate([mine, none], 1), jnp.concatenate([none, mine], 1)], 0
            ).astype(jnp.bfloat16)
            for n in range(4):
                row = b * 64 + n * 16
                wave_mat[phase, n, row : row + 16] = pair
    for load in loads[1:4]:
        load.wait()

    def scatter(target, place, value):
        for n in range(2):
            target[n, pl.ds(place, frames, stride=8), :] = value[:, n * 128 : n * 128 + 128]

    for d in range(3):
        x = pos_ref[d]
        scatter(coords, 2 * d, (x >> 7).astype(jnp.float32) * (1.0 / 128.0))
        scatter(coords, 2 * d + 1, (x & 127).astype(jnp.float32) * (1.0 / 16384.0))
    for d in (6, 7):
        scatter(coords, d, jnp.zeros((frames, atoms), jnp.float32))
    species_b = species_ref[...].astype(jnp.float32)
    species_a = 1.0 - species_b
    for q in range(4):
        for n, spec in enumerate((species_a, species_b)):
            if q == 0:
                rows = jnp.broadcast_to(spec, (frames, atoms))
            else:
                rows = vel_ref[q - 1] * spec
            scatter(kinds, 2 * q + n, rows)

    def trig(turn):
        rest = turn - jnp.round(turn)
        z = rest * rest
        zz = z * z
        half_sin = rest * ((z + SIN_A) * (zz + SIN_B) + SIN_C)
        half_cos = (z + COS_A) * (zz + COS_B) + COS_C
        return half_sin * half_sin, half_sin * half_cos

    def pair_copy(phase):
        return pltpu.make_async_remote_copy(
            src_ref=modes.at[phase, other],
            dst_ref=from_pair.at[phase],
            send_sem=pair_send.at[phase],
            recv_sem=pair_recv.at[phase],
            device_id=(me, other),
            device_id_type=pl.DeviceIdType.MESH,
        )

    def peer_copy(phase, hop):
        local = lax.rem(place + hop, part)
        return pltpu.make_async_remote_copy(
            src_ref=summed.at[phase, local],
            dst_ref=signals.at[me],
            send_sem=peer_send.at[phase, hop],
            recv_sem=peer_recv.at[me],
            device_id=(trade(phase * part + local), core),
            device_id_type=pl.DeviceIdType.MESH,
        )

    def arrival(hop):
        peer = lax.rem(me + hop, tm_size)
        return pltpu.make_async_remote_copy(
            src_ref=summed.at[0, 0],
            dst_ref=signals.at[peer],
            send_sem=peer_send.at[0, 0],
            recv_sem=peer_recv.at[peer],
            device_id=(peer, core),
            device_id_type=pl.DeviceIdType.MESH,
        )

    def reduce_and_send(phase):
        pair_copy(phase).wait_recv()
        summed[phase] = modes[phase, core] + from_pair[phase]
        for hop in range(1, part):
            peer_copy(phase, hop).start()

        @pl.when(place // part == phase)
        def _():
            signals[me] = summed[phase, lax.rem(place, part)]

        @pl.when(place // part != phase)
        def _():
            peer_copy(phase, 0).start()

    half = atoms // 2

    for tg in range(groups):
        for n in range(2):
            block = jnp.concatenate(
                [coords[n, m * 128 + tg * 64 : m * 128 + tg * 64 + 64, :] for m in range(2)], 0
            )
            places[tg, n * 128 : n * 128 + 128] = block.T.astype(jnp.bfloat16)

    def find_turn(phase, unit, slot):
        turns[slot] = jnp.dot(
            places[unit // 4],
            wave_mat[phase, unit % 4],
            preferred_element_type=jnp.float32,
        )

    def one_unit(phase, unit, slot):
        lefts, totals = [], []
        for k in range(2):
            stack = []
            for m in range(2):
                rows = pl.ds(unit * 16 + m * 128 + k * 8, 8)
                kind = jnp.concatenate([kinds[0, rows, :], kinds[1, rows, :]], 1)
                totals.append(jnp.sum(kind, axis=1, keepdims=True))
                kind_high = kind.astype(jnp.bfloat16).astype(jnp.float32)
                stack += [kind_high, kind - kind_high]
            lefts.append(jnp.concatenate(stack, 0).astype(jnp.bfloat16))
        sums = [None, None]
        for n in range(2):
            drop, sine = trig(turns[slot, n * half : n * half + half])
            for k in range(2):
                left = lefts[k][:, n * half : n * half + half]
                both = jnp.concatenate(
                    [v[:, k * 128 : k * 128 + 128] for v in (drop, sine)], 1
                )
                product = jnp.dot(
                    jnp.concatenate([left, left], 1),
                    jnp.concatenate(split(both), 0),
                    preferred_element_type=jnp.float32,
                )
                sums[k] = product if n == 0 else sums[k] + product
        for k in range(2):
            rows = pl.ds(unit * 16 + k * 8, 8)
            here = sums[k][:8] + sums[k][8:16]
            later = sums[k][16:24] + sums[k][24:]
            total = jnp.where(low_lane, totals[2 * k], totals[2 * k + 1])
            drop = jnp.where(low_lane, here[:, :128], later[:, :128])
            sine = jnp.where(low_lane, here[:, 128:], later[:, 128:])
            acc[phase % 2, 0, rows, :] = total - (SIN_SCALE * SIN_SCALE) * drop
            acc[phase % 2, 1, rows, :] = (SIN_SCALE * COS_SCALE) * sine

    def one_phase(phase):
        if phase == 0:
            find_turn(0, 0, 0)

        def step(index):
            if phase == 1 and index == steps - 1:
                pl.semaphore_wait(barrier, tm_size)
                pair_copy(0).start()
            if phase == 2 and index == 0:
                reduce_and_send(0)
            if phase >= 2 and index == steps - 1:
                reduce_and_send(phase - 1)
            for k in range(STEP):
                unit = index * STEP + k
                if unit + 1 < units:
                    find_turn(phase, unit + 1, (k + 1) % 2)
                elif phase + 1 < PHASES:
                    find_turn(phase + 1, 0, (k + 1) % 2)
                one_unit(phase, unit, k % 2)

        for index in range(steps):
            step(index)
        rows = []
        for c in range(2):
            parts = [acc[phase % 2, c, pl.ds(n, GROUP, stride=8), :] for n in range(8)]
            rows += parts[:2]
            for n in range(2):
                rows.append(
                    factor[phase, 0:1] * parts[2 + n]
                    + factor[phase, 2:3] * parts[4 + n]
                    + factor[phase, 4:5] * parts[6 + n]
                )
        packed = jnp.concatenate(rows, 0).T.reshape(2, part, 2, 8, 128)
        for n in range(2):
            for m in range(2):
                modes[phase, n, :, m] = packed[m, :, n]

        if phase >= 1:
            pair_copy(phase).start()

    for phase in range(PHASES):
        one_phase(phase)
    reduce_and_send(PHASES - 1)
    for load in loads[4:]:
        load.wait()
    for hop in range(1, tm_size):
        arrival(hop).wait_recv()

    tiles = signals[...].reshape(frame_total // 128, 8, 8, 128)
    wide = frame_total // 128 * 8
    group_lane = lax.broadcasted_iota(jnp.int32, (wide, 128), 1) // 16
    turned = [
        pltpu.roll(tiles[:, p].reshape(wide, 128), 16 * p, 1) if p else tiles[:, p].reshape(wide, 128)
        for p in range(8)
    ]
    rows = []
    for m in range(8):
        picked = turned[0]
        for p in range(1, 8):
            picked = jnp.where(group_lane == (m + p) % 8, turned[p], picked)
        if m:
            picked = pltpu.roll(picked, 128 - 16 * m, 1)
        rows.append(
            jnp.concatenate([picked[v * 8 : v * 8 + 8] for v in range(frame_total // 128)], 1)
        )
    signal = jnp.concatenate(rows, 0)
    blocks = frame_total // BLOCK
    high, low = split(
        jnp.concatenate([signal[:, n * BLOCK : n * BLOCK + BLOCK] for n in range(blocks)], 0)
    )
    spectra = jnp.dot(
        jnp.concatenate([high, low, high], 1), table[...], preferred_element_type=jnp.float32
    )
    lane = lax.broadcasted_iota(jnp.int32, (8, BLOCK), 1)
    first = lane == 0
    flip = jnp.where(lane % 2 == 0, 1.0, -1.0)

    def spectrum(block, c, g, spec):
        row = block * 64 + (c * 4 + g * 2 + spec) * 8
        return spectra[row : row + 8, :BLOCK], spectra[row : row + 8, BLOCK:]

    out_rows = [[], []]
    for g in range(2):
        for a, b in ((0, 0), (0, 1), (1, 1)):
            shifts = []
            for shift in range(3):
                even = odd = imag = None
                for c in range(2):
                    for n in range(blocks - shift):
                        cos_a, sin_a = spectrum(n + shift, c, g, a)
                        cos_b, sin_b = spectrum(n, c, g, b)
                        terms = (cos_a * cos_b, sin_a * sin_b, sin_a * cos_b - cos_a * sin_b)
                        if even is None:
                            even, odd, imag = terms
                        else:
                            even, odd, imag = even + terms[0], odd + terms[1], imag + terms[2]
                shifts.append(
                    (
                        jnp.where(first, even, 2.0 * (even + odd)),
                        jnp.where(first, odd, 2.0 * imag),
                    )
                )
            for n in range(2):
                out_rows[n].append(
                    jnp.concatenate(
                        [now + flip * later for now, later in zip(shifts[n], shifts[n + 1])], 1
                    )
                )
    high, low = split(jnp.concatenate(out_rows[0] + out_rows[1], 0))
    both = jnp.dot(
        jnp.concatenate([high, low], 0), back[...], preferred_element_type=jnp.float32
    )
    corr = both[:96, :BLOCK] + both[96:, :BLOCK] + both[:96, BLOCK:]
    lag = lax.broadcasted_iota(jnp.int32, (1, BLOCK), 1)
    for n in range(2):
        norm = 1.0 / (
            (frame_total - n * BLOCK - lag).astype(jnp.float32)
            * jnp.float32(2 * BLOCK * 2 * atoms)
        )
        result[n] = (corr[n * 48 : n * 48 + 48] * norm).reshape(6, 8, BLOCK)
    swap = pltpu.make_async_remote_copy(
        src_ref=result.at[other],
        dst_ref=result_in,
        send_sem=last_send,
        recv_sem=last_recv,
        device_id=(me, other),
        device_id_type=pl.DeviceIdType.MESH,
    )
    swap.start()
    out_ref[:, pl.ds(pl.multiple_of(core * 8, 8), 8), :] = result[core]
    for phase in range(PHASES):
        pair_copy(phase).wait_send()
        for hop in range(1, part):
            peer_copy(phase, hop).wait_send()

        @pl.when(place // part != phase)
        def _():
            peer_copy(phase, 0).wait_send()

    swap.wait()
    out_ref[:, pl.ds(pl.multiple_of(other * 8, 8), 8), :] = result_in[...]


def per_device_fused(tm_size, positions, velocities, species, wave_vectors):
    frames, atoms = positions.shape[1:]
    waves = wave_vectors.shape[1]
    groups = frames // GROUP
    frame_total = frames * tm_size
    lag_here = frame_total // 4
    vmem = pl.BlockSpec(memory_space=pltpu.VMEM)
    dma = pltpu.SemaphoreType.DMA
    return pl.pallas_call(
        lambda *refs: fused_kernel(tm_size, *refs),
        name="scattering",
        out_shape=jax.ShapeDtypeStruct((6, 16, lag_here), jnp.float32),
        in_specs=[pl.BlockSpec(memory_space=pltpu.HBM)] * 6,
        out_specs=vmem,
        scratch_shapes=[
            pltpu.VMEM(positions.shape, jnp.int32),
            pltpu.VMEM(velocities.shape, jnp.float32),
            pltpu.VMEM((1, atoms), jnp.int32),
            pltpu.VMEM(wave_vectors.shape, jnp.int32),
            pltpu.VMEM((3 * BLOCK, 2 * BLOCK), jnp.bfloat16),
            pltpu.VMEM((2 * BLOCK, 2 * BLOCK), jnp.bfloat16),
            pltpu.VMEM((PHASES, 4, 8 * GROUP, waves), jnp.bfloat16),
            pltpu.VMEM((2, 8 * frames, 128), jnp.float32),
            pltpu.VMEM((groups, atoms, 8 * GROUP), jnp.bfloat16),
            pltpu.VMEM((PHASES, 8, 128), jnp.float32),
            pltpu.VMEM((2, 8 * frames, 128), jnp.float32),
            pltpu.VMEM((2, atoms, waves), jnp.float32),
            pltpu.VMEM((2, 2, 8 * GROUP, 128), jnp.float32),
            pltpu.VMEM((PHASES, 2, tm_size // PHASES, groups, 8, 128), jnp.float32),
            pltpu.VMEM((PHASES, tm_size // PHASES, groups, 8, 128), jnp.float32),
            pltpu.VMEM((PHASES, tm_size // PHASES, groups, 8, 128), jnp.float32),
            pltpu.VMEM((tm_size, groups, 8, 128), jnp.float32),
            pltpu.VMEM((2, 6, 8, lag_here), jnp.float32),
            pltpu.VMEM((6, 8, lag_here), jnp.float32),
            dma((6,)),
            dma((PHASES,)),
            dma((PHASES,)),
            dma((PHASES, tm_size // PHASES)),
            dma((tm_size,)),
            dma,
            dma,
        ],
        compiler_params=pltpu.CompilerParams(
            collective_id=0, has_side_effects=True, vmem_limit_bytes=48 << 20
        ),
    )(
        *(
            pltpu.with_memory_space_constraint(operand, pltpu.HBM)
            for operand in (
                positions,
                velocities,
                species.reshape(1, atoms),
                wave_vectors,
                *(jnp.asarray(table) for table in dft_tables(BLOCK)),
            )
        )
    )


def solution(mesh):
    tm_size = mesh.shape["tm"]
    atom_size = mesh.shape["atom"]

    def per_device(positions, velocities, species, wave_vectors):
        frames, atoms = positions.shape[1:]
        waves = wave_vectors.shape[1]
        fits = (
            tm_size == 16
            and atom_size == 2
            and frames == 2 * GROUP
            and atoms == 256
            and waves == 256
        )
        if fits:
            return per_device_fused(tm_size, positions, velocities, species, wave_vectors)
        return per_device_general(positions, velocities, species, wave_vectors)

    return jax.shard_map(
        per_device,
        mesh=mesh,
        in_specs=(P(None, "tm", "atom"), P(None, "tm", "atom"), P("atom"), P()),
        out_specs=P(None, "tm", "atom"),
        check_vma=False,
    )
```
